256 devices in a mesh: wide: 32 (over y, z), narrow: 8 (over x, core).
Axes of the slice: x: 4, y: 4, z: 8, core: 2. Of those that a mesh axis runs over, the one named last changes fastest.
Arguments:
- activations: bfloat16 [1024, 28672], P('wide', 'narrow'), may hold values from -6 to 6
- out_grads: bfloat16 [1024, 8192], P('wide'), may hold values from -6 to 6
- basis_in: bfloat16 [28672, 28672], P('narrow', 'wide'), may hold values from -0.03125 to 0.03125
- basis_out: bfloat16 [8192, 8192], P('wide', 'narrow'), may hold values from -0.0625 to 0.0625
- eigenvalues: bfloat16 [8192, 28672], P('narrow', 'wide'), may hold values from 0.29882812 to 10
- queries: bfloat16 [2, 8192, 28672], P(None, 'narrow', 'wide'), may hold values from -0.00036621094 to 0.00036621094
- doc_ids: int32 [1024], replicated, may hold values from 0 to 63, never falling along the last dimension, each value on 1 to 32 neighbouring positions
Outputs:
- scores: float32 [64, 2], replicated
The draws below stay inside these ranges and needn't reach their ends.
Inputs may be any that keep to these rules, and one draw needn't show every extreme that they name: `doc_ids`: document numbers never fall along the tokens; each document has 1 to 32 tokens.
All inputs are finite; a program needn't handle non-finite values.
Results may differ from the reference program's by a relative error of at most 0.0051.
Values may be sent and summed in bfloat16 or wider, within the bound.
No kernel may reach another device: no remote copies, remote signals or barrier semaphores. Data moves between devices by JAX's collectives and lax.ppermute only.
A program may use at most 128 MiB of HBM per device.

```python
import math
import jax
import jax.numpy as jnp
import numpy as np
from jax import lax

D = 8192
FF = 28672
NQ = 2
TOKENS = 1024
DOCS = 64
DOC_MOST = 32


def shard_levels(stream_key, dims, split, smallest, largest):
    level = 1.0
    for position, shards_of in split:
        heights = jax.random.uniform(jax.random.fold_in(jax.random.fold_in(stream_key, 6), position), (shards_of,), jnp.float32, smallest / len(split), largest / len(split))
        level = level * jnp.repeat(jnp.exp(heights), dims[position] // shards_of).reshape((-1,) + (1,) * (len(dims) - 1 - position))
    return level


def profile(number_of, total, bound, skew):
    loads = [(1 << 20) // math.isqrt(standing ** skew) + 1 for standing in range(2, number_of + 1)]
    rest, counts = total - bound - (number_of - 1), [1] * (number_of - 1)
    while rest > 0:
        candidates = [i for i in range(number_of - 1) if counts[i] < bound]
        pool, budget = sum([loads[i] for i in candidates]), rest
        for i in candidates:
            extra = min(bound - counts[i], max(1, budget * loads[i] // pool), rest)
            counts[i] = counts[i] + extra
            rest = rest - extra
    return np.array([bound] + counts)


def uneven(stream_key, number_of, total, bound, slope):
    if number_of == 2:
        one = jax.random.randint(stream_key, (), max(1, total - bound), min(bound, total - 1) + 1)
        return jnp.stack([one, total - one])
    lengths = jnp.asarray(profile(number_of, total, bound, slope), jnp.int32)
    couples = (number_of - 1) // 2
    donor, sink = lengths[1:1 + 2 * couples:2], lengths[2:2 + 2 * couples:2]
    margin = jnp.minimum(donor - 1, bound - sink)
    passed = jax.random.randint(jax.random.fold_in(stream_key, 1), (couples,), 0, 1 << 20) % (margin + 1)
    lengths = lengths.at[1:1 + 2 * couples:2].set(donor - passed).at[2:2 + 2 * couples:2].set(sink + passed)
    return lengths[jax.random.permutation(jax.random.fold_in(stream_key, 2), number_of)]


def centred(stream_key, shape, deviation, most, cuts=(), held_as=jnp.bfloat16):
    factor_of = shard_levels(stream_key, shape, cuts, -0.22, 0.18) if cuts else 1.0
    values = jax.random.normal(stream_key, shape, jnp.float32) * deviation * factor_of
    return jnp.minimum(jnp.maximum(values, -most), most).astype(held_as)


def setup_inputs(seed: int = 0) -> dict:
    keys = jax.random.split(jax.random.key(seed), 8)
    activations = centred(keys[0], (TOKENS, FF), 1.0, 6.0, ((0, 32), (1, 8)))
    out_grads = centred(keys[1], (TOKENS, D), 1.0, 6.0, ((0, 32),))
    basis_in = centred(keys[2], (FF, FF), FF ** -0.5, 0.03125, ((0, 8), (1, 32)))
    basis_out = centred(keys[3], (D, D), D ** -0.5, 0.0625, ((0, 32), (1, 8)))
    eigenvalues = jnp.clip(jnp.exp(math.log(10.0) - 3.5104718 * jax.random.uniform(keys[4], (D, FF), jnp.float32) ** shard_levels(keys[4], (D, FF), ((0, 8), (1, 32)), -0.2, 0.2)), 0.29882812, 10.0).astype(jnp.bfloat16)
    queries = centred(keys[5], (NQ, D, FF), (D * FF) ** -0.5, 0.00036621094, ((1, 8), (2, 32)))
    doc_ids = jnp.searchsorted(jnp.cumsum(uneven(keys[6], DOCS, TOKENS, DOC_MOST, 2)), jnp.arange(TOKENS), side="right").astype(jnp.int32)
    return dict(activations=activations, out_grads=out_grads, basis_in=basis_in, basis_out=basis_out, eigenvalues=eigenvalues, queries=queries, doc_ids=doc_ids)


DAMPING = 0.1


def reference(activations, out_grads, basis_in, basis_out, eigenvalues, queries, doc_ids):
    rot_acts = jnp.dot(activations, basis_in, preferred_element_type=jnp.float32).astype(jnp.bfloat16)
    rot_grads = jnp.dot(out_grads, basis_out, preferred_element_type=jnp.float32).astype(jnp.bfloat16)
    precond = (queries.astype(jnp.float32) / (eigenvalues.astype(jnp.float32)[None] + DAMPING)).astype(jnp.bfloat16)
    acts_float = rot_acts.astype(jnp.float32)

    def per_query(scaled):
        mixed_rows = jnp.dot(rot_grads, scaled, preferred_element_type=jnp.float32)
        return jnp.sum(mixed_rows * acts_float, axis=1)

    token_scores = lax.map(per_query, precond)
    member = (doc_ids[None, :] == jnp.arange(DOCS, dtype=jnp.int32)[:, None]).astype(jnp.float32)
    return jnp.dot(member, token_scores.T, precision=lax.Precision.HIGHEST)
```

```python
import jax
import jax.numpy as jnp
from jax import lax
from jax.sharding import Mesh
from jax.sharding import PartitionSpec as P

WIDE = ("y", "z")
NARROW = ("x", "c")
ALL = ("y", "z", "x", "c")
SIZE = {"y": 4, "z": 8, "x": 4, "c": 2}
DOCS = 64
DAMPING = 0.1
F32 = jnp.float32
BF16 = jnp.bfloat16


def shift(value, axis, hops):
    size = SIZE[axis]
    return lax.ppermute(value, axis, [(i, (i + hops) % size) for i in range(size)])


def ring(chunk, axis):
    size = SIZE[axis]
    half = size // 2
    got = {0: chunk}
    ahead = back = chunk
    for step in range(1, half):
        ahead, back = shift(ahead, axis, 1), shift(back, axis, -1)
        got[step], got[size - step] = ahead, back
    cut = chunk.shape[1] // 2
    far = [shift(ahead[:, :cut], axis, 1), shift(back[:, cut:], axis, -1)]
    got[half] = jnp.concatenate(far, axis=1)
    return [got[i] for i in range(size)]


def gather_rows(local):
    rows = local.shape[0] // 2
    upper = jnp.concatenate(ring(local[:rows], "z"), axis=0)
    lower = jnp.concatenate(ring(local[rows:], "y"), axis=0)
    return ring(upper, "y"), ring(lower, "z")


def gathered_ids(doc_ids, y, z):
    blocks = doc_ids.reshape(4, 8, 2, 16)
    back_y = lax.rem(y + 4 - jnp.arange(4), 4)
    back_z = lax.rem(z + 8 - jnp.arange(8), 8)
    rolled = blocks[back_y][:, back_z]
    upper = rolled[:, :, 0].reshape(512)
    lower = rolled[:, :, 1].transpose(1, 0, 2).reshape(512)
    return jnp.concatenate([upper, lower])


def over_narrow(partial):
    rows, cols = partial.shape
    parts = lax.all_to_all(partial.reshape(8, rows // 8, cols), NARROW, 0, 0)
    share = jnp.sum(parts.astype(F32), axis=0).astype(BF16)
    copies = jnp.broadcast_to(share[None], (8, rows // 8, cols))
    return lax.all_to_all(copies, NARROW, 0, 0).reshape(rows, cols)


def rotated_grads(out_grads, basis_out):
    cols = basis_out.shape[1]
    rows = out_grads.reshape(32, 4, 8, 256).transpose(2, 0, 1, 3)
    rows = lax.all_to_all(rows, "z", 0, 0)
    bases = ring(basis_out, "y")
    y = lax.axis_index("y")
    total = 0.0
    for back in range(4):
        part = lax.dynamic_index_in_dim(rows, lax.rem(y + 4 - back, 4), 2, keepdims=False)
        total = total + jnp.dot(part.reshape(256, 256), bases[back], preferred_element_type=F32)
    parts = lax.all_to_all(total.astype(BF16).reshape(8, 32, cols), "z", 0, 0)
    return jnp.sum(parts.astype(F32), axis=0).astype(BF16)


def shards(activations, out_grads, basis_in, basis_out, eigenvalues, queries, doc_ids):
    y, z = lax.axis_index("y"), lax.axis_index("z")
    upper, lower = gather_rows(activations)
    acts = jnp.concatenate(upper + lower, axis=0)
    partial_acts = jnp.dot(acts, basis_in, preferred_element_type=F32).astype(BF16)
    rot_acts = over_narrow(partial_acts)
    upper, lower = gather_rows(rotated_grads(out_grads, basis_out))
    rot_grads = jnp.concatenate(upper + lower, axis=0)
    precond = (queries.astype(F32) / (eigenvalues.astype(F32)[None] + DAMPING)).astype(BF16)
    mixed = jnp.einsum("ti,qij->qtj", rot_grads, precond, preferred_element_type=F32)
    token_part = jnp.sum(mixed * rot_acts.astype(F32)[None], axis=2)
    ids = gathered_ids(doc_ids, y, z)
    member = (ids[None, :] == jnp.arange(DOCS, dtype=jnp.int32)[:, None]).astype(F32)
    partial_docs = jnp.dot(member, token_part.T, precision=lax.Precision.HIGHEST)
    copies = jnp.broadcast_to(partial_docs.reshape(1, DOCS * 2), (256, DOCS * 2))
    return jnp.sum(lax.all_to_all(copies, ALL, 0, 0, tiled=True), axis=0).reshape(DOCS, 2)


def solution(mesh):
    finer = Mesh(mesh.devices.reshape(4, 8, 4, 2), ALL)
    in_specs = (
        P(WIDE, NARROW),
        P(WIDE, None),
        P(NARROW, WIDE),
        P(WIDE, NARROW),
        P(NARROW, WIDE),
        P(None, NARROW, WIDE),
        P(),
    )
    return jax.shard_map(
        shards, mesh=finer, in_specs=in_specs, out_specs=P(), check_vma=False
    )
```

```python
import functools

import jax
import jax.numpy as jnp
from jax import lax
from jax.experimental import pallas as pl
from jax.experimental.pallas import tpu as pltpu
from jax.sharding import Mesh
from jax.sharding import PartitionSpec as P

WIDE = ("y", "z")
NARROW = ("x", "c")
ALL = ("y", "z", "x", "c")
SIZE = {"y": 4, "z": 8, "x": 4, "c": 2}
DOCS = 64
DAMPING = 0.1
F32 = jnp.float32
BF16 = jnp.bfloat16
STEP = 512


def shift(value, axis, hops):
    size = SIZE[axis]
    return lax.ppermute(value, axis, [(i, (i + hops) % size) for i in range(size)])


def ring(chunk, axis):
    size = SIZE[axis]
    half = size // 2
    got = [(0, 0, chunk)]
    ahead = back = chunk
    for step in range(1, half):
        ahead, back = shift(ahead, axis, 1), shift(back, axis, -1)
        got += [(step, 0, ahead), (size - step, 0, back)]
    cut = chunk.shape[1] // 2
    got += [(half, 0, shift(ahead[:, :cut], axis, 1)), (half, cut, shift(back[:, cut:], axis, -1))]
    return got


def spread(value, axes, size):
    return lax.all_to_all(jnp.broadcast_to(value[None], (size,) + value.shape), axes, 0, 0)


def rotate_kernel(places, size, rows, here, *refs):
    chunks, (basis, out, lhs, rhs, total, chunk_sems, basis_sems) = refs[: len(places)], refs[len(places) :]
    steps = basis.shape[0] // STEP
    loads = []
    for n, ((back, first, width), chunk) in enumerate(zip(places, chunks)):
        slot = lax.rem(here[0] + size - back, size) * rows
        into = lhs.at[pl.ds(pl.multiple_of(slot, rows), rows), pl.ds(first, width)]
        loads.append(pltpu.make_async_copy(chunk, into, chunk_sems.at[n]))

    def basis_load(k):
        span = pl.ds(pl.multiple_of(k * STEP, STEP), STEP)
        return pltpu.make_async_copy(basis.at[span], rhs.at[k], basis_sems.at[k])

    for load in loads:
        load.start()
    for k in range(steps):
        basis_load(k).start()
    for load in loads:
        load.wait()
    basis_load(0).wait()
    total[...] = jnp.dot(lhs[:, :STEP], rhs[0], preferred_element_type=F32)

    @pl.loop(1, steps)
    def _(k):
        basis_load(k).wait()
        part = lhs[:, pl.ds(pl.multiple_of(k * STEP, STEP), STEP)]
        total[...] += jnp.dot(part, rhs[k], preferred_element_type=F32)

    out[...] = total[...].astype(BF16)


def rotate(chunks, axis, basis, here):
    size = SIZE[axis]
    rows = chunks[0][2].shape[0]
    depth, cols = basis.shape
    places = [(back, first, chunk.shape[1]) for back, first, chunk in chunks]
    count = size * rows
    steps = depth // STEP
    return pl.pallas_call(
        functools.partial(rotate_kernel, places, size, rows),
        out_shape=jax.ShapeDtypeStruct((count, cols), BF16),
        in_specs=[pl.BlockSpec(memory_space=pltpu.SMEM)]
        + [pl.BlockSpec(memory_space=pl.ANY)] * (len(places) + 1),
        out_specs=pl.BlockSpec(memory_space=pltpu.VMEM),
        scratch_shapes=[
            pltpu.VMEM((count, depth), BF16),
            pltpu.VMEM((steps, STEP, cols), BF16),
            pltpu.VMEM((count, cols), F32),
            pltpu.SemaphoreType.DMA((len(places),)),
            pltpu.SemaphoreType.DMA((steps,)),
        ],
        cost_estimate=pl.CostEstimate(
            flops=2 * count * depth * cols,
            bytes_accessed=2 * (count * depth + depth * cols + count * cols),
            transcendentals=0,
        ),
        compiler_params=pltpu.CompilerParams(vmem_limit_bytes=24 << 20),
        name="rotate_" + axis,
    )(here.reshape(1), *[chunk for _, _, chunk in chunks], basis)


def score_kernel(grads, precond, acts, ids, out):
    mixed = jnp.dot(grads[...], precond[0], preferred_element_type=F32)
    token = jnp.sum(mixed * acts[...].astype(F32), axis=1, keepdims=True)
    docs = lax.broadcasted_iota(jnp.int32, (token.shape[0], 128), 1)
    out[0] = jnp.sum(jnp.where(ids[...] == docs, token, 0.0), axis=0, keepdims=True)


def score(grads, precond, acts, ids):
    tokens, rows = grads.shape
    count, _, cols = precond.shape
    return pl.pallas_call(
        score_kernel,
        grid=(count,),
        out_shape=jax.ShapeDtypeStruct((count, 1, 128), F32),
        in_specs=[
            pl.BlockSpec((tokens, rows), lambda q: (0, 0)),
            pl.BlockSpec((1, rows, cols), lambda q: (q, 0, 0)),
            pl.BlockSpec((tokens, cols), lambda q: (0, 0)),
            pl.BlockSpec((tokens, 1), lambda q: (0, 0)),
        ],
        out_specs=pl.BlockSpec((1, 1, 128), lambda q: (q, 0, 0)),
        cost_estimate=pl.CostEstimate(
            flops=2 * count * tokens * rows * cols,
            bytes_accessed=2 * (tokens * rows + count * rows * cols + tokens * cols),
            transcendentals=0,
        ),
        compiler_params=pltpu.CompilerParams(vmem_limit_bytes=24 << 20),
        name="score",
    )(grads, precond, acts, ids.reshape(tokens, 1))


def over_narrow(partial):
    rows, cols = partial.shape
    parts = lax.all_to_all(partial.reshape(8, rows // 8, cols), NARROW, 0, 0)
    share = jnp.sum(parts.astype(F32), axis=0).astype(BF16)
    return spread(share, NARROW, 8).reshape(rows, cols)


def rotated_grads(out_grads, basis_out):
    cols = basis_out.shape[1]
    basis = spread(basis_out, "y", 4).reshape(1024, cols)
    rows = out_grads.reshape(32, 4, 8, 256).transpose(2, 0, 1, 3)
    rows = lax.all_to_all(rows, "z", 0, 0).reshape(256, 1024)
    partial = jnp.dot(rows, basis, preferred_element_type=F32).astype(BF16)
    parts = lax.all_to_all(partial.reshape(8, 32, cols), "z", 0, 0)
    return jnp.sum(parts.astype(F32), axis=0).astype(BF16)


def shards(activations, out_grads, basis_in, basis_out, eigenvalues, queries, doc_ids):
    y, z = lax.axis_index("y"), lax.axis_index("z")
    low = spread(activations[16:], "y", 4).reshape(64, -1)
    high = spread(activations[:16], "z", 8).reshape(128, -1)
    low = over_narrow(rotate(ring(low, "z"), "z", basis_in, z))
    high = over_narrow(rotate(ring(high, "y"), "y", basis_in, y))
    grads = rotated_grads(out_grads, basis_out)
    low_grads = spread(spread(grads[16:], "y", 4).reshape(64, -1), "z", 8).reshape(512, -1)
    high_grads = spread(spread(grads[:16], "z", 8).reshape(128, -1), "y", 4).reshape(512, -1)
    precond = (queries.astype(F32) / (eigenvalues.astype(F32)[None] + DAMPING)).astype(BF16)
    ids = doc_ids.reshape(4, 8, 2, 16)
    docs = score(low_grads, precond, low, ids[:, :, 1].transpose(1, 0, 2))
    docs += score(high_grads, precond, high, ids[:, :, 0])
    total = jnp.sum(spread(docs[:, 0, :DOCS].reshape(1, 2 * DOCS), ALL, 256), axis=0)
    return total.reshape(2, DOCS).T


def solution(mesh):
    finer = Mesh(mesh.devices.reshape(4, 8, 4, 2), ALL)
    in_specs = (
        P(WIDE, NARROW),
        P(WIDE, None),
        P(NARROW, WIDE),
        P(WIDE, NARROW),
        P(NARROW, WIDE),
        P(None, NARROW, WIDE),
        P(),
    )
    return jax.shard_map(
        shards, mesh=finer, in_specs=in_specs, out_specs=P(), check_vma=False
    )
```

```python
import functools

import jax
import jax.numpy as jnp
from jax import lax
from jax.experimental import pallas as pl
from jax.experimental.pallas import tpu as pltpu
from jax.sharding import Mesh
from jax.sharding import PartitionSpec as P

WIDE = ("y", "z")
NARROW = ("x", "c")
ALL = ("y", "z", "x", "c")
SIZE = {"y": 4, "z": 8, "x": 4, "c": 2}
DOCS = 64
DAMPING = 0.1
F32 = jnp.float32
BF16 = jnp.bfloat16
STEP = 512
SPLIT = 3072


def shift(value, axis, hops):
    size = SIZE[axis]
    return lax.ppermute(value, axis, [(i, (i + hops) % size) for i in range(size)])


def ring(chunk, axis):
    size = SIZE[axis]
    half = size // 2
    got = [(0, 0, chunk)]
    ahead = back = chunk
    for step in range(1, half):
        ahead, back = shift(ahead, axis, 1), shift(back, axis, -1)
        got += [(step, 0, ahead), (size - step, 0, back)]
    cut = chunk.shape[1] // 2
    got += [(half, 0, shift(ahead[:, :cut], axis, 1)), (half, cut, shift(back[:, cut:], axis, -1))]
    return got


def spread(value, axes, size):
    return lax.all_to_all(jnp.broadcast_to(value[None], (size,) + value.shape), axes, 0, 0)


def join_kernel(places, rows, here, *refs):
    chunks, out = refs[: len(places)], refs[-1]
    for back, chunk in zip(places, chunks):
        row = pl.multiple_of(lax.rem(here[0] + len(places) - back, len(places)) * rows, rows)
        out[pl.ds(row, rows), :] = chunk[...]


def join(value, axis, here):
    rows, cols = value.shape
    size = SIZE[axis]
    places = [0, 1, size - 1] + list(range(2, size - 1))
    chunks = [value] + [shift(value, axis, back) for back in places[1:]]
    return pl.pallas_call(
        functools.partial(join_kernel, places, rows),
        out_shape=jax.ShapeDtypeStruct((size * rows, cols), BF16),
        in_specs=[pl.BlockSpec(memory_space=pltpu.SMEM)] + [pl.BlockSpec(memory_space=pltpu.VMEM)] * size,
        out_specs=pl.BlockSpec(memory_space=pltpu.VMEM),
        cost_estimate=pl.CostEstimate(flops=0, bytes_accessed=4 * size * rows * cols, transcendentals=0),
        name="join",
    )(here, *chunks)


def rotate_kernel(y_places, z_places, here, *refs):
    count = len(y_places) + len(z_places)
    chunks, (own, other, out, lhs, rhs, total, chunk_sems, basis_sems) = refs[:count], refs[count:]
    half = own.shape[0]
    steps = half // STEP
    loads = []

    def load(chunk, row, rows, first, width):
        into = lhs.at[pl.ds(pl.multiple_of(row, rows), rows), pl.ds(first, width)]
        loads.append(pltpu.make_async_copy(chunk, into, chunk_sems.at[len(loads)]))

    for (back, first, width), chunk in zip(y_places, chunks):
        load(chunk, lax.rem(here[0] + 4 - back, 4) * 128, 128, first, width)
    for (back, first, width), chunk in zip(z_places, chunks[len(y_places) :]):
        for y in range(4):
            row = y * 128 + lax.rem(here[1] + 8 - back, 8) * 16
            load(chunk.at[pl.ds(y * 16, 16)], row, 16, SPLIT + first, width)

    def basis_load(basis, k, at):
        span = pl.ds(pl.multiple_of(k * STEP, STEP), STEP)
        return pltpu.make_async_copy(basis.at[span], rhs.at[at], basis_sems.at[at])

    for n in loads:
        n.start()
    for basis, base in ((own, 0), (other, steps)):
        for k in range(steps):
            basis_load(basis, k, base + k).start()
    for n in loads:
        n.wait()
    total[...] = jnp.zeros_like(total)

    @pl.loop(0, steps)
    def _(k):
        basis_load(own, 0, 2 * k).wait()
        basis_load(own, 0, 2 * k + 1).wait()
        part = lhs[:, pl.ds(pl.multiple_of(k * 2 * STEP, 2 * STEP), 2 * STEP)]
        both = rhs[pl.ds(2 * k, 2)].reshape(2 * STEP, rhs.shape[2])
        total[...] += jnp.dot(part, both, preferred_element_type=F32)

    out[...] = total[...].astype(BF16)


def rotate(y_chunks, z_chunks, own, other, here):
    depth, cols = own.shape
    y_places, z_places = (
        [(back, first, chunk.shape[1]) for back, first, chunk in chunks] for chunks in (y_chunks, z_chunks)
    )
    count = 512
    steps = 2 * depth // STEP
    return pl.pallas_call(
        functools.partial(rotate_kernel, y_places, z_places),
        out_shape=jax.ShapeDtypeStruct((count, cols), BF16),
        in_specs=[pl.BlockSpec(memory_space=pltpu.SMEM)]
        + [pl.BlockSpec(memory_space=pl.ANY)] * (len(y_places) + len(z_places))
        + [pl.BlockSpec(memory_space=pltpu.HBM)] * 2,
        out_specs=pl.BlockSpec(memory_space=pltpu.VMEM),
        scratch_shapes=[
            pltpu.VMEM((count, 2 * depth), BF16),
            pltpu.VMEM((steps, STEP, cols), BF16),
            pltpu.VMEM((count, cols), F32),
            pltpu.SemaphoreType.DMA((len(y_places) + 4 * len(z_places),)),
            pltpu.SemaphoreType.DMA((steps,)),
        ],
        cost_estimate=pl.CostEstimate(
            flops=4 * count * depth * cols,
            bytes_accessed=2 * (2 * count * depth + 2 * depth * cols + count * cols),
            transcendentals=0,
        ),
        compiler_params=pltpu.CompilerParams(vmem_limit_bytes=32 << 20),
        name="rotate",
    )(here, *[chunk for _, _, chunk in y_chunks + z_chunks], own, other)


def score_kernel(grads, own, other, acts, ids, out):
    half = own.shape[1]
    mixed = jnp.dot(grads[:, :half], own[0], preferred_element_type=F32)
    mixed += jnp.dot(grads[:, half:], other[0], preferred_element_type=F32)
    token = jnp.sum(mixed * acts[...].astype(F32), axis=1, keepdims=True)
    docs = lax.broadcasted_iota(jnp.int32, (token.shape[0], 128), 1)
    out[0] = jnp.sum(jnp.where(ids[...] == docs, token, 0.0), axis=0, keepdims=True)


def score(grads, own, other, acts, ids):
    tokens, rows = grads.shape
    count, half, cols = own.shape
    return pl.pallas_call(
        score_kernel,
        grid=(count,),
        out_shape=jax.ShapeDtypeStruct((count, 1, 128), F32),
        in_specs=[
            pl.BlockSpec((tokens, rows), lambda q: (0, 0)),
            pl.BlockSpec((1, half, cols), lambda q: (q, 0, 0)),
            pl.BlockSpec((1, half, cols), lambda q: (q, 0, 0)),
            pl.BlockSpec((tokens, cols), lambda q: (0, 0)),
            pl.BlockSpec((tokens, 1), lambda q: (0, 0)),
        ],
        out_specs=pl.BlockSpec((1, 1, 128), lambda q: (q, 0, 0)),
        cost_estimate=pl.CostEstimate(
            flops=2 * count * tokens * rows * cols,
            bytes_accessed=2 * (tokens * rows + count * rows * cols + tokens * cols),
            transcendentals=0,
        ),
        compiler_params=pltpu.CompilerParams(vmem_limit_bytes=24 << 20),
        name="score",
    )(grads, own, other, acts, ids.reshape(tokens, 1))


def over_x(partial):
    rows, cols = partial.shape
    parts = lax.all_to_all(partial.reshape(4, rows // 4, cols), "x", 0, 0)
    share = jnp.sum(parts.astype(F32), axis=0).astype(BF16)
    return spread(share, "x", 4).reshape(rows, cols)


def swap(value):
    return shift(value, "c", 1)


def shards(activations, out_grads, basis_in, basis_out, eigenvalues, queries, doc_ids):
    y, z, c = (lax.axis_index(axis) for axis in "yzc")
    here = jnp.stack([y, z])
    other_in = swap(basis_in)
    mine = lax.dynamic_slice_in_dim(activations, c * 16, 16)
    theirs = swap(lax.dynamic_slice_in_dim(activations, (1 - c) * 16, 16))
    low = join(jnp.concatenate([mine[:, SPLIT:], theirs], axis=1), "y", here)
    rows = lax.dynamic_slice_in_dim(out_grads, c * 16, 16).reshape(16, 4, 8, 256)
    rows = rows.transpose(2, 0, 1, 3).reshape(8, 16, 1024)
    copies = jnp.broadcast_to(mine[None, :, :SPLIT], (8, 16, SPLIT))
    sent = lax.all_to_all(jnp.concatenate([copies, rows], axis=2), "z", 0, 0)
    high = sent[:, :, :SPLIT].reshape(128, SPLIT)
    rows = sent[:, :, SPLIT:].reshape(128, 1024)
    partial_acts = rotate(ring(high, "y"), ring(low, "z"), basis_in, other_in, here)
    rot_acts = over_x(partial_acts)

    basis = lax.all_gather(basis_out, "y", axis=0, tiled=True)
    partial = [jnp.dot(part, basis, preferred_element_type=F32).astype(BF16) for part in (rows, swap(rows))]
    partial = jnp.stack([part.reshape(8, 16, 1024) for part in partial], axis=1)
    parts = lax.all_to_all(partial, "z", 0, 0)
    grads = jnp.sum(parts.astype(F32), axis=0).astype(BF16)
    grads = jnp.concatenate([grads[0], swap(grads[1])], axis=1)
    grads = spread(grads, "z", 8).reshape(128, 2048)
    rot_grads = lax.all_gather(grads, "y", axis=0, tiled=True)
    precond = (queries.astype(F32) / (eigenvalues.astype(F32)[None] + DAMPING)).astype(BF16)
    ids = lax.dynamic_index_in_dim(doc_ids.reshape(32, 2, 16), c, 1, keepdims=False)
    docs = score(rot_grads, precond, swap(precond), rot_acts, ids)
    total = jnp.sum(spread(docs[:, 0, :DOCS].reshape(1, 2 * DOCS), ALL, 256), axis=0)
    return total.reshape(2, DOCS).T


def solution(mesh):
    finer = Mesh(mesh.devices.reshape(4, 8, 4, 2), ALL)
    in_specs = (
        P(WIDE, NARROW),
        P(WIDE, None),
        P(NARROW, WIDE),
        P(WIDE, NARROW),
        P(NARROW, WIDE),
        P(None, NARROW, WIDE),
        P(),
    )
    return jax.shard_map(
        shards, mesh=finer, in_specs=in_specs, out_specs=P(), check_vma=False
    )
```

```python
import functools

import jax
import jax.numpy as jnp
from jax import lax
from jax.experimental import pallas as pl
from jax.experimental.pallas import tpu as pltpu
from jax.sharding import Mesh
from jax.sharding import PartitionSpec as P

WIDE = ("y", "z")
NARROW = ("x", "c")
ALL = ("y", "z", "x", "c")
SIZE = {"y": 4, "z": 8, "x": 4, "c": 2}
DOCS = 64
DAMPING = 0.1
F32 = jnp.float32
BF16 = jnp.bfloat16
STEP = 512
SPLIT = 3072


def shift(value, axis, hops):
    size = SIZE[axis]
    return lax.ppermute(value, axis, [(i, (i + hops) % size) for i in range(size)])


def ring(chunk, axis):
    size = SIZE[axis]
    half = size // 2
    got = [(0, 0, chunk)]
    ahead = back = chunk
    for step in range(1, half):
        ahead, back = shift(ahead, axis, 1), shift(back, axis, -1)
        got += [(step, 0, ahead), (size - step, 0, back)]
    cut = chunk.shape[1] // 2
    got += [(half, 0, shift(ahead[:, :cut], axis, 1)), (half, cut, shift(back[:, cut:], axis, -1))]
    return got


def spread(value, axes, size):
    return lax.all_to_all(jnp.broadcast_to(value[None], (size,) + value.shape), axes, 0, 0)


def join_kernel(places, rows, here, *refs):
    chunks, out = refs[: len(places)], refs[-1]
    for back, chunk in zip(places, chunks):
        row = pl.multiple_of(lax.rem(here[0] + len(places) - back, len(places)) * rows, rows)
        out[pl.ds(row, rows), :] = chunk[...]


def join(value, axis, here):
    rows, cols = value.shape
    size = SIZE[axis]
    places = [0, 1, size - 1] + list(range(2, size - 1))
    chunks = [value] + [shift(value, axis, back) for back in places[1:]]
    return pl.pallas_call(
        functools.partial(join_kernel, places, rows),
        out_shape=jax.ShapeDtypeStruct((size * rows, cols), BF16),
        in_specs=[pl.BlockSpec(memory_space=pltpu.SMEM)] + [pl.BlockSpec(memory_space=pltpu.VMEM)] * size,
        out_specs=pl.BlockSpec(memory_space=pltpu.VMEM),
        cost_estimate=pl.CostEstimate(flops=0, bytes_accessed=4 * size * rows * cols, transcendentals=0),
        name="join",
    )(here, *chunks)


def rotate_kernel(y_places, z_places, here, *refs):
    count = len(y_places) + len(z_places)
    chunks, (own, other, out, lhs, rhs, total, chunk_sems, basis_sems) = refs[:count], refs[count:]
    half = own.shape[0]
    steps = half // STEP
    loads = []

    def load(chunk, row, rows, first, width):
        into = lhs.at[pl.ds(pl.multiple_of(row, rows), rows), pl.ds(first, width)]
        loads.append(pltpu.make_async_copy(chunk, into, chunk_sems.at[len(loads)]))

    for (back, first, width), chunk in zip(y_places, chunks):
        load(chunk, lax.rem(here[0] + 4 - back, 4) * 128, 128, first, width)
    for (back, first, width), chunk in zip(z_places, chunks[len(y_places) :]):
        for y in range(4):
            row = y * 128 + lax.rem(here[1] + 8 - back, 8) * 16
            load(chunk.at[pl.ds(y * 16, 16)], row, 16, SPLIT + first, width)

    def basis_load(basis, k, at):
        span = pl.ds(pl.multiple_of(k * STEP, STEP), STEP)
        return pltpu.make_async_copy(basis.at[span], rhs.at[at], basis_sems.at[at])

    for n in loads:
        n.start()
    for basis, base in ((own, 0), (other, steps)):
        for k in range(steps):
            basis_load(basis, k, base + k).start()
    for n in loads:
        n.wait()
    total[...] = jnp.zeros_like(total)

    @pl.loop(0, steps)
    def _(k):
        basis_load(own, 0, 2 * k).wait()
        basis_load(own, 0, 2 * k + 1).wait()
        part = lhs[:, pl.ds(pl.multiple_of(k * 2 * STEP, 2 * STEP), 2 * STEP)]
        both = rhs[pl.ds(2 * k, 2)].reshape(2 * STEP, rhs.shape[2])
        total[...] += jnp.dot(part, both, preferred_element_type=F32)

    out[...] = total[...].astype(BF16)


def rotate(y_chunks, z_chunks, own, other, here):
    depth, cols = own.shape
    y_places, z_places = (
        [(back, first, chunk.shape[1]) for back, first, chunk in chunks] for chunks in (y_chunks, z_chunks)
    )
    count = 512
    steps = 2 * depth // STEP
    return pl.pallas_call(
        functools.partial(rotate_kernel, y_places, z_places),
        out_shape=jax.ShapeDtypeStruct((count, cols), BF16),
        in_specs=[pl.BlockSpec(memory_space=pltpu.SMEM)]
        + [pl.BlockSpec(memory_space=pl.ANY)] * (len(y_places) + len(z_places))
        + [pl.BlockSpec(memory_space=pltpu.HBM)] * 2,
        out_specs=pl.BlockSpec(memory_space=pltpu.VMEM),
        scratch_shapes=[
            pltpu.VMEM((count, 2 * depth), BF16),
            pltpu.VMEM((steps, STEP, cols), BF16),
            pltpu.VMEM((count, cols), F32),
            pltpu.SemaphoreType.DMA((len(y_places) + 4 * len(z_places),)),
            pltpu.SemaphoreType.DMA((steps,)),
        ],
        cost_estimate=pl.CostEstimate(
            flops=4 * 4 * count * depth * cols,
            bytes_accessed=2 * (2 * count * depth + 2 * depth * cols + count * cols),
            transcendentals=0,
        ),
        compiler_params=pltpu.CompilerParams(vmem_limit_bytes=56 << 20),
        name="rotate",
    )(here, *[chunk for _, _, chunk in y_chunks + z_chunks], own, other)


def score_kernel(grads, own, other, acts, ids, out):
    half = own.shape[1]
    mixed = jnp.dot(grads[:, :half], own[0], preferred_element_type=F32)
    mixed += jnp.dot(grads[:, half:], other[0], preferred_element_type=F32)
    token = jnp.sum(mixed * acts[...].astype(F32), axis=1, keepdims=True)
    docs = lax.broadcasted_iota(jnp.int32, (token.shape[0], 128), 1)
    out[0] = jnp.sum(jnp.where(ids[...] == docs, token, 0.0), axis=0, keepdims=True)


def score(grads, own, other, acts, ids):
    tokens, rows = grads.shape
    count, half, cols = own.shape
    return pl.pallas_call(
        score_kernel,
        grid=(count,),
        out_shape=jax.ShapeDtypeStruct((count, 1, 128), F32),
        in_specs=[
            pl.BlockSpec((tokens, rows), lambda q: (0, 0)),
            pl.BlockSpec((1, half, cols), lambda q: (q, 0, 0)),
            pl.BlockSpec((1, half, cols), lambda q: (q, 0, 0)),
            pl.BlockSpec((tokens, cols), lambda q: (0, 0)),
            pl.BlockSpec((tokens, 1), lambda q: (0, 0)),
        ],
        out_specs=pl.BlockSpec((1, 1, 128), lambda q: (q, 0, 0)),
        cost_estimate=pl.CostEstimate(
            flops=2 * count * tokens * rows * cols,
            bytes_accessed=2 * (tokens * rows + count * rows * cols + tokens * cols),
            transcendentals=0,
        ),
        compiler_params=pltpu.CompilerParams(vmem_limit_bytes=24 << 20),
        name="score",
    )(grads, own, other, acts, ids.reshape(tokens, 1))


def over_x(partial):
    rows, cols = partial.shape
    parts = lax.all_to_all(partial.reshape(4, rows // 4, cols), "x", 0, 0)
    share = jnp.sum(parts.astype(F32), axis=0).astype(BF16)
    return spread(share, "x", 4).reshape(rows, cols)


def swap(value):
    return shift(value, "c", 1)


def shards(activations, out_grads, basis_in, basis_out, eigenvalues, queries, doc_ids):
    y, z, c = (lax.axis_index(axis) for axis in "yzc")
    here = jnp.stack([y, z])
    other_in = swap(basis_in)
    mine = lax.dynamic_slice_in_dim(activations, c * 16, 16)
    theirs = swap(lax.dynamic_slice_in_dim(activations, (1 - c) * 16, 16))
    low = join(jnp.concatenate([mine[:, SPLIT:], theirs], axis=1), "y", here)
    rows = lax.dynamic_slice_in_dim(out_grads, c * 16, 16).reshape(16, 4, 8, 256)
    rows = rows.transpose(2, 0, 1, 3).reshape(8, 16, 1024)
    copies = jnp.broadcast_to(mine[None, :, :SPLIT], (8, 16, SPLIT))
    sent = lax.all_to_all(jnp.concatenate([copies, rows], axis=2), "z", 0, 0)
    high = sent[:, :, :SPLIT].reshape(128, SPLIT)
    rows = sent[:, :, SPLIT:].reshape(128, 1024)
    partial_acts = rotate(ring(high, "y"), ring(low, "z"), basis_in, other_in, here)
    rot_acts = over_x(partial_acts)

    basis = lax.all_gather(basis_out, "y", axis=0, tiled=True)
    partial = [jnp.dot(part, basis, preferred_element_type=F32).astype(BF16) for part in (rows, swap(rows))]
    partial = jnp.stack([part.reshape(8, 16, 1024) for part in partial], axis=1)
    parts = lax.all_to_all(partial, "z", 0, 0)
    grads = jnp.sum(parts.astype(F32), axis=0).astype(BF16)
    grads = jnp.concatenate([grads[0], swap(grads[1])], axis=1)
    grads = spread(grads, "z", 8).reshape(128, 2048)
    rot_grads = lax.all_gather(grads, "y", axis=0, tiled=True)
    precond = (queries.astype(F32) / (eigenvalues.astype(F32)[None] + DAMPING)).astype(BF16)
    ids = lax.dynamic_index_in_dim(doc_ids.reshape(32, 2, 16), c, 1, keepdims=False)
    docs = score(rot_grads, precond, swap(precond), rot_acts, ids)
    total = jnp.sum(spread(docs[:, 0, :DOCS].reshape(1, 2 * DOCS), ALL, 256), axis=0)
    return total.reshape(2, DOCS).T


def solution(mesh):
    finer = Mesh(mesh.devices.reshape(4, 8, 4, 2), ALL)
    in_specs = (
        P(WIDE, NARROW),
        P(WIDE, None),
        P(NARROW, WIDE),
        P(WIDE, NARROW),
        P(NARROW, WIDE),
        P(None, NARROW, WIDE),
        P(),
    )
    return jax.shard_map(
        shards, mesh=finer, in_specs=in_specs, out_specs=P(), check_vma=False
    )
```

```python
import functools

import jax
import jax.numpy as jnp
from jax import lax
from jax.experimental import pallas as pl
from jax.experimental.pallas import tpu as pltpu
from jax.sharding import Mesh
from jax.sharding import PartitionSpec as P

WIDE = ("y", "z")
NARROW = ("x", "c")
ALL = ("y", "z", "x", "c")
SIZE = {"y": 4, "z": 8, "x": 4, "c": 2}
DOCS = 64
DAMPING = 0.1
F32 = jnp.float32
BF16 = jnp.bfloat16
STEP = 512


def shift(value, axis, hops):
    size = SIZE[axis]
    return lax.ppermute(value, axis, [(i, (i + hops) % size) for i in range(size)])


def ring(chunk, axis):
    size = SIZE[axis]
    half = size // 2
    got = [(0, 0, chunk)]
    ahead = back = chunk
    for step in range(1, half):
        ahead, back = shift(ahead, axis, 1), shift(back, axis, -1)
        got += [(step, 0, ahead), (size - step, 0, back)]
    cut = chunk.shape[1] // 2
    got += [(half, 0, shift(ahead[:, :cut], axis, 1)), (half, cut, shift(back[:, cut:], axis, -1))]
    return got


def spread(value, axes, size):
    return lax.all_to_all(jnp.broadcast_to(value[None], (size,) + value.shape), axes, 0, 0)


def join_kernel(places, rows, here, *refs):
    chunks, out = refs[: len(places)], refs[-1]
    for back, chunk in zip(places, chunks):
        row = pl.multiple_of(lax.rem(here[0] + len(places) - back, len(places)) * rows, rows)
        out[pl.ds(row, rows), :] = chunk[...]


def join(value, axis, here):
    rows, cols = value.shape
    size = SIZE[axis]
    places = [0, 1, size - 1] + list(range(2, size - 1))
    chunks = [value] + [shift(value, axis, back) for back in places[1:]]
    return pl.pallas_call(
        functools.partial(join_kernel, places, rows),
        out_shape=jax.ShapeDtypeStruct((size * rows, cols), BF16),
        in_specs=[pl.BlockSpec(memory_space=pltpu.SMEM)] + [pl.BlockSpec(memory_space=pltpu.VMEM)] * size,
        out_specs=pl.BlockSpec(memory_space=pltpu.VMEM),
        cost_estimate=pl.CostEstimate(flops=0, bytes_accessed=4 * size * rows * cols, transcendentals=0),
        name="join",
    )(here, *chunks)


def rotate_kernel(places, axis, summed, here, *refs):
    count = len(places)
    chunks, basis, refs = refs[:count], refs[count], refs[count + 1 :]
    before, (out, lhs, rhs, total, chunk_sems, basis_sems) = refs[:summed], refs[summed:]
    steps = basis.shape[0] // STEP
    loads = []

    def load(chunk, row, rows, first, width):
        into = lhs.at[pl.ds(pl.multiple_of(row, rows), rows), pl.ds(first, width)]
        loads.append(pltpu.make_async_copy(chunk, into, chunk_sems.at[len(loads)]))

    for (back, first, width), chunk in zip(places, chunks):
        if axis == "y":
            load(chunk, lax.rem(here[0] + 4 - back, 4) * 128, 128, first, width)
        else:
            for y in range(4):
                row = y * 128 + lax.rem(here[1] + 8 - back, 8) * 16
                load(chunk.at[pl.ds(y * 16, 16)], row, 16, first, width)

    def basis_load(k):
        span = pl.ds(pl.multiple_of(k * STEP, STEP), STEP)
        return pltpu.make_async_copy(basis.at[span], rhs.at[k], basis_sems.at[k])

    for n in loads:
        n.start()
    for k in range(steps):
        basis_load(k).start()
    total[...] = before[0][...] if summed else jnp.zeros_like(total)
    for n in loads:
        n.wait()

    @pl.loop(0, steps)
    def _(k):
        basis_load(k).wait()
        part = lhs[:, pl.ds(pl.multiple_of(k * STEP, STEP), STEP)]
        total[...] += jnp.dot(part, rhs[k], preferred_element_type=F32)

    out[...] = total[...].astype(out.dtype)


def rotate(chunks, axis, basis, here, dtype, before=()):
    depth, cols = basis.shape
    places = [(back, first, chunk.shape[1]) for back, first, chunk in chunks]
    count = 512
    steps = depth // STEP
    copies = len(places) * (1 if axis == "y" else 4)
    return pl.pallas_call(
        functools.partial(rotate_kernel, places, axis, len(before)),
        out_shape=jax.ShapeDtypeStruct((count, cols), dtype),
        in_specs=[pl.BlockSpec(memory_space=pltpu.SMEM)]
        + [pl.BlockSpec(memory_space=pl.ANY)] * len(places)
        + [pl.BlockSpec(memory_space=pltpu.HBM)]
        + [pl.BlockSpec(memory_space=pltpu.VMEM)] * len(before),
        out_specs=pl.BlockSpec(memory_space=pltpu.VMEM),
        scratch_shapes=[
            pltpu.VMEM((count, depth), BF16),
            pltpu.VMEM((steps, STEP, cols), BF16),
            pltpu.VMEM((count, cols), F32),
            pltpu.SemaphoreType.DMA((copies,)),
            pltpu.SemaphoreType.DMA((steps,)),
        ],
        cost_estimate=pl.CostEstimate(
            flops=(4 if axis == "y" else 8) * 2 * count * depth * cols,
            bytes_accessed=2 * (count * depth + depth * cols + count * cols),
            transcendentals=0,
        ),
        compiler_params=pltpu.CompilerParams(vmem_limit_bytes=48 << 20),
        name="rotate_" + axis,
    )(here, *[chunk for _, _, chunk in chunks], basis, *before)


def score_kernel(grads, own, other, acts, ids, out):
    half = own.shape[1]
    mixed = jnp.dot(grads[:, :half], own[0], preferred_element_type=F32)
    mixed += jnp.dot(grads[:, half:], other[0], preferred_element_type=F32)
    token = jnp.sum(mixed * acts[...].astype(F32), axis=1, keepdims=True)
    docs = lax.broadcasted_iota(jnp.int32, (token.shape[0], 128), 1)
    out[0] = jnp.sum(jnp.where(ids[...] == docs, token, 0.0), axis=0, keepdims=True)


def score(grads, own, other, acts, ids):
    tokens, rows = grads.shape
    count, half, cols = own.shape
    return pl.pallas_call(
        score_kernel,
        grid=(count,),
        out_shape=jax.ShapeDtypeStruct((count, 1, 128), F32),
        in_specs=[
            pl.BlockSpec((tokens, rows), lambda q: (0, 0)),
            pl.BlockSpec((1, half, cols), lambda q: (q, 0, 0)),
            pl.BlockSpec((1, half, cols), lambda q: (q, 0, 0)),
            pl.BlockSpec((tokens, cols), lambda q: (0, 0)),
            pl.BlockSpec((tokens, 1), lambda q: (0, 0)),
        ],
        out_specs=pl.BlockSpec((1, 1, 128), lambda q: (q, 0, 0)),
        cost_estimate=pl.CostEstimate(
            flops=2 * count * tokens * rows * cols,
            bytes_accessed=2 * (tokens * rows + count * rows * cols + tokens * cols),
            transcendentals=0,
        ),
        compiler_params=pltpu.CompilerParams(vmem_limit_bytes=24 << 20),
        name="score",
    )(grads, own, other, acts, ids.reshape(tokens, 1))


def over_x(partial):
    rows, cols = partial.shape
    parts = lax.all_to_all(partial.reshape(4, rows // 4, cols), "x", 0, 0)
    share = jnp.sum(parts.astype(F32), axis=0).astype(BF16)
    return spread(share, "x", 4).reshape(rows, cols)


def swap(value):
    return shift(value, "c", 1)


def shards(activations, out_grads, basis_in, basis_out, eigenvalues, queries, doc_ids):
    y, z, c = (lax.axis_index(axis) for axis in "yzc")
    here = jnp.stack([y, z])
    other_in = swap(basis_in)
    mine = lax.dynamic_slice_in_dim(activations, c * 16, 16)
    theirs = swap(lax.dynamic_slice_in_dim(activations, (1 - c) * 16, 16))
    low = join(theirs, "y", here)
    rows = lax.dynamic_slice_in_dim(out_grads, c * 16, 16).reshape(16, 4, 8, 256)
    rows = rows.transpose(2, 0, 1, 3).reshape(8, 16, 1024)
    copies = jnp.broadcast_to(mine[None], (8,) + mine.shape)
    sent = lax.all_to_all(jnp.concatenate([copies, rows], axis=2), "z", 0, 0)
    high = sent[:, :, : mine.shape[1]].reshape(128, -1)
    rows = sent[:, :, mine.shape[1] :].reshape(128, 1024)
    partial_acts = rotate(ring(high, "y"), "y", basis_in, here, F32)
    partial_acts = rotate(ring(low, "z"), "z", other_in, here, BF16, (partial_acts,))
    rot_acts = over_x(partial_acts)

    basis = lax.all_gather(basis_out, "y", axis=0, tiled=True)
    partial = [jnp.dot(part, basis, preferred_element_type=F32).astype(BF16) for part in (rows, swap(rows))]
    partial = jnp.stack([part.reshape(8, 16, 1024) for part in partial], axis=1)
    parts = lax.all_to_all(partial, "z", 0, 0)
    grads = jnp.sum(parts.astype(F32), axis=0).astype(BF16)
    grads = jnp.concatenate([grads[0], swap(grads[1])], axis=1)
    grads = spread(grads, "z", 8).reshape(128, 2048)
    rot_grads = lax.all_gather(grads, "y", axis=0, tiled=True)
    precond = (queries.astype(F32) / (eigenvalues.astype(F32)[None] + DAMPING)).astype(BF16)
    ids = lax.dynamic_index_in_dim(doc_ids.reshape(32, 2, 16), c, 1, keepdims=False)
    docs = score(rot_grads, precond, swap(precond), rot_acts, ids)
    total = jnp.sum(spread(docs[:, 0, :DOCS].reshape(1, 2 * DOCS), ALL, 256), axis=0)
    return total.reshape(2, DOCS).T


def solution(mesh):
    finer = Mesh(mesh.devices.reshape(4, 8, 4, 2), ALL)
    in_specs = (
        P(WIDE, NARROW),
        P(WIDE, None),
        P(NARROW, WIDE),
        P(WIDE, NARROW),
        P(NARROW, WIDE),
        P(None, NARROW, WIDE),
        P(),
    )
    return jax.shard_map(
        shards, mesh=finer, in_specs=in_specs, out_specs=P(), check_vma=False
    )
```

```python
import functools

import jax
import jax.numpy as jnp
from jax import lax
from jax.experimental import pallas as pl
from jax.experimental.pallas import tpu as pltpu
from jax.sharding import Mesh
from jax.sharding import PartitionSpec as P

WIDE = ("y", "z")
NARROW = ("x", "c")
ALL = ("y", "z", "x", "c")
SIZE = {"y": 4, "z": 8, "x": 4, "c": 2}
DOCS = 64
DAMPING = 0.1
F32 = jnp.float32
BF16 = jnp.bfloat16
STEP = 512
SPLIT = 4096


def shift(value, axis, hops):
    size = SIZE[axis]
    return lax.ppermute(value, axis, [(i, (i + hops) % size) for i in range(size)])


def ring(chunk, axis):
    size = SIZE[axis]
    half = size // 2
    got = [(0, 0, chunk)]
    ahead = back = chunk
    for step in range(1, half):
        ahead, back = shift(ahead, axis, 1), shift(back, axis, -1)
        got += [(step, 0, ahead), (size - step, 0, back)]
    cut = chunk.shape[1] // 2
    got += [(half, 0, shift(ahead[:, :cut], axis, 1)), (half, cut, shift(back[:, cut:], axis, -1))]
    return got


def spread(value, axes, size):
    return lax.all_to_all(jnp.broadcast_to(value[None], (size,) + value.shape), axes, 0, 0)


def join_kernel(places, rows, here, *refs):
    chunks, out = refs[: len(places)], refs[-1]
    for back, chunk in zip(places, chunks):
        row = pl.multiple_of(lax.rem(here[0] + len(places) - back, len(places)) * rows, rows)
        out[pl.ds(row, rows), :] = chunk[...]


PLACES = (0, 1, 3, 2)


def direct(value):
    return [value] + [shift(value, "y", back) for back in PLACES[1:]]


def join(value, here):
    rows, cols = value.shape
    return pl.pallas_call(
        functools.partial(join_kernel, PLACES, rows),
        out_shape=jax.ShapeDtypeStruct((4 * rows, cols), BF16),
        in_specs=[pl.BlockSpec(memory_space=pltpu.SMEM)] + [pl.BlockSpec(memory_space=pltpu.VMEM)] * 4,
        out_specs=pl.BlockSpec(memory_space=pltpu.VMEM),
        cost_estimate=pl.CostEstimate(flops=0, bytes_accessed=16 * rows * cols, transcendentals=0),
        name="join",
    )(here, *direct(value))


def project_kernel(here, own, other, first, second, third, fourth, precond, out):
    for half, rows in enumerate((own, other)):
        total = 0.0
        for back, basis in zip(PLACES, (first, second, third, fourth)):
            slot = pl.multiple_of(lax.rem(here[0] + 4 - back, 4) * 256, 256)
            total += jnp.dot(rows[:, pl.ds(slot, 256)], basis[...], preferred_element_type=F32)
        out[:, half] = total.astype(BF16).reshape(8, 16, 1024)


def project(own, other, bases, precond, here):
    vmem = pl.BlockSpec(memory_space=pltpu.VMEM)
    return pl.pallas_call(
        project_kernel,
        out_shape=jax.ShapeDtypeStruct((8, 2, 16, 1024), BF16),
        in_specs=[pl.BlockSpec(memory_space=pltpu.SMEM)] + [vmem] * 6 + [pl.BlockSpec(memory_space=pl.ANY)],
        out_specs=vmem,
        cost_estimate=pl.CostEstimate(flops=2**29, bytes_accessed=2**22, transcendentals=0),
        compiler_params=pltpu.CompilerParams(vmem_limit_bytes=16 << 20),
        name="project",
    )(here, own, other, *bases, precond)


def damp_kernel(queries, eigenvalues, _, out):
    damped = eigenvalues[...].astype(F32) + DAMPING
    for q in range(2):
        out[q] = (queries[q].astype(F32) / damped).astype(BF16)


def damp(queries, eigenvalues, ready):
    count, rows, cols = queries.shape
    return pl.pallas_call(
        damp_kernel,
        grid=(rows // 128,),
        out_shape=jax.ShapeDtypeStruct((count, rows, cols), BF16),
        in_specs=[
            pl.BlockSpec((count, 128, cols), lambda i: (0, i, 0)),
            pl.BlockSpec((128, cols), lambda i: (i, 0)),
            pl.BlockSpec(memory_space=pl.ANY),
        ],
        out_specs=pl.BlockSpec((count, 128, cols), lambda i: (0, i, 0)),
        cost_estimate=pl.CostEstimate(
            flops=2 * count * rows * cols, bytes_accessed=10 * rows * cols, transcendentals=0
        ),
        compiler_params=pltpu.CompilerParams(vmem_limit_bytes=8 << 20),
        name="damp",
    )(queries, eigenvalues, ready)


def rotate_kernel(places, axis, spans, summed, here, *refs):
    count = len(places)
    chunks, bases, refs = refs[:count], refs[count : count + len(spans)], refs[count + len(spans) :]
    before, (_, out, lhs, rhs, total, chunk_sems, basis_sems) = refs[:summed], refs[summed:]
    steps = rhs.shape[0]
    loads = []

    def load(chunk, row, rows, first, width):
        into = lhs.at[pl.ds(pl.multiple_of(row, rows), rows), pl.ds(first, width)]
        loads.append(pltpu.make_async_copy(chunk, into, chunk_sems.at[len(loads)]))

    for (back, first, width), chunk in zip(places, chunks):
        if axis == "y":
            load(chunk, lax.rem(here[0] + 4 - back, 4) * 128, 128, first, width)
        else:
            for y in range(4):
                row = y * 128 + lax.rem(here[1] + 8 - back, 8) * 16
                load(chunk.at[pl.ds(y * 16, 16)], row, 16, first, width)

    def basis_load(basis, row, k):
        return pltpu.make_async_copy(basis.at[pl.ds(row, STEP)], rhs.at[k], basis_sems.at[k])

    for n in loads:
        n.start()
    k = 0
    for basis, (first, last) in zip(bases, spans):
        for row in range(first, last, STEP):
            basis_load(basis, row, k).start()
            k += 1
    total[...] = before[0][...] if summed else jnp.zeros_like(total)
    for n in loads:
        n.wait()

    @pl.loop(0, steps)
    def _(k):
        basis_load(bases[0], 0, k).wait()
        part = lhs[:, pl.ds(pl.multiple_of(k * STEP, STEP), STEP)]
        total[...] += jnp.dot(part, rhs[k], preferred_element_type=F32)

    out[...] = total[...].astype(out.dtype)


def rotate(chunks, axis, bases, here, dtype, ready, before=()):
    spans = [span for _, span in bases]
    depth, cols = sum(last - first for first, last in spans), bases[0][0].shape[1]
    places = [(back, first, chunk.shape[1]) for back, first, chunk in chunks]
    count = 512
    steps = depth // STEP
    copies = len(places) * (1 if axis == "y" else 4)
    return pl.pallas_call(
        functools.partial(rotate_kernel, places, axis, spans, len(before)),
        out_shape=jax.ShapeDtypeStruct((count, cols), dtype),
        in_specs=[pl.BlockSpec(memory_space=pltpu.SMEM)]
        + [pl.BlockSpec(memory_space=pl.ANY)] * len(places)
        + [pl.BlockSpec(memory_space=pltpu.HBM)] * len(bases)
        + [pl.BlockSpec(memory_space=pltpu.VMEM)] * len(before)
        + [pl.BlockSpec(memory_space=pl.ANY)],
        out_specs=pl.BlockSpec(memory_space=pltpu.VMEM),
        scratch_shapes=[
            pltpu.VMEM((count, depth), BF16),
            pltpu.VMEM((steps, STEP, cols), BF16),
            pltpu.VMEM((count, cols), F32),
            pltpu.SemaphoreType.DMA((copies,)),
            pltpu.SemaphoreType.DMA((steps,)),
        ],
        cost_estimate=pl.CostEstimate(
            flops=(2 if axis == "y" else 2) * 2 * count * depth * cols,
            bytes_accessed=2 * (count * depth + depth * cols + count * cols),
            transcendentals=0,
        ),
        compiler_params=pltpu.CompilerParams(vmem_limit_bytes=48 << 20),
        name="rotate_" + axis,
    )(here, *[chunk for _, _, chunk in chunks], *[basis for basis, _ in bases], *before, ready)


def score_kernel(here, first, second, third, fourth, own, other, acts, ids, out, grads, sems):
    @pl.when(pl.program_id(0) == 0)
    def _():
        loads = []
        for n, (back, chunk) in enumerate(zip(PLACES, (first, second, third, fourth))):
            row = pl.multiple_of(lax.rem(here[0] + 4 - back, 4) * 128, 128)
            loads.append(pltpu.make_async_copy(chunk, grads.at[pl.ds(row, 128)], sems.at[n]))
        for load in loads:
            load.start()
        for load in loads:
            load.wait()

    half = own.shape[1]
    mixed = jnp.dot(grads[:, :half], own[0], preferred_element_type=F32)
    mixed += jnp.dot(grads[:, half:], other[0], preferred_element_type=F32)
    token = jnp.sum(mixed * acts[...].astype(F32), axis=1, keepdims=True)
    docs = lax.broadcasted_iota(jnp.int32, (token.shape[0], 128), 1)
    out[0] = jnp.sum(jnp.where(ids[...] == docs, token, 0.0), axis=0, keepdims=True)


def score(chunks, own, other, acts, ids, here):
    tokens, cols = acts.shape
    count, half, _ = own.shape
    return pl.pallas_call(
        score_kernel,
        grid=(count,),
        out_shape=jax.ShapeDtypeStruct((count, 1, 128), F32),
        in_specs=[pl.BlockSpec(memory_space=pltpu.SMEM)]
        + [pl.BlockSpec(memory_space=pl.ANY)] * 4
        + [
            pl.BlockSpec((1, half, cols), lambda q: (q, 0, 0)),
            pl.BlockSpec((1, half, cols), lambda q: (q, 0, 0)),
            pl.BlockSpec((tokens, cols), lambda q: (0, 0)),
            pl.BlockSpec((tokens, 1), lambda q: (0, 0)),
        ],
        out_specs=pl.BlockSpec((1, 1, 128), lambda q: (q, 0, 0)),
        scratch_shapes=[pltpu.VMEM((tokens, 2 * half), BF16), pltpu.SemaphoreType.DMA((4,))],
        cost_estimate=pl.CostEstimate(
            flops=4 * count * tokens * half * cols,
            bytes_accessed=2 * (2 * tokens * half + 2 * count * half * cols + tokens * cols),
            transcendentals=0,
        ),
        compiler_params=pltpu.CompilerParams(vmem_limit_bytes=48 << 20),
        name="score",
    )(here, *chunks, own, other, acts, ids.reshape(tokens, 1))


def after_kernel(value, ready, out):
    pass


def after(value, ready):
    anywhere = pl.BlockSpec(memory_space=pl.ANY)
    return pl.pallas_call(
        after_kernel,
        out_shape=jax.ShapeDtypeStruct(value.shape, value.dtype),
        in_specs=[anywhere, anywhere],
        out_specs=anywhere,
        input_output_aliases={0: 0},
        name="after",
    )(value, ready)


def over_x(partial):
    rows, cols = partial.shape
    parts = lax.all_to_all(partial.reshape(4, rows // 4, cols), "x", 0, 0)
    share = jnp.sum(parts.astype(F32), axis=0).astype(BF16)
    return spread(share, "x", 4).reshape(rows, cols)


def swap(value):
    return shift(value, "c", 1)


def shards(activations, out_grads, basis_in, basis_out, eigenvalues, queries, doc_ids):
    y, z, c = (lax.axis_index(axis) for axis in "yzc")
    here = jnp.stack([y, z])
    other_in = swap(basis_in)
    mine = lax.dynamic_slice_in_dim(activations, c * 16, 16)
    theirs = swap(lax.dynamic_slice_in_dim(activations, (1 - c) * 16, 16))
    bases = direct(basis_out)
    extra = SPLIT - mine.shape[1]
    low = join(theirs[:, extra:], here)
    precond = damp(queries, eigenvalues, low)
    rows = lax.dynamic_slice_in_dim(out_grads, c * 16, 16).reshape(16, 4, 8, 256)
    rows = rows.transpose(2, 0, 1, 3).reshape(8, 16, 1024)
    mine = jnp.concatenate([mine, theirs[:, :extra]], axis=1)
    copies = jnp.broadcast_to(mine[None], (8,) + mine.shape)
    sent = lax.all_to_all(jnp.concatenate([copies, rows], axis=2), "z", 0, 0)
    high = sent[:, :, :SPLIT].reshape(128, -1)
    rows = sent[:, :, SPLIT:].reshape(128, 1024)
    half = basis_in.shape[0]
    high_bases = ((basis_in, (0, half)), (other_in, (0, extra)))[: 1 + (extra > 0)]
    parts = lax.all_to_all(project(rows, swap(rows), bases, precond, here), "z", 0, 0)
    partial_acts = rotate(ring(high, "y"), "y", high_bases, here, F32, parts)
    grads = jnp.sum(parts.astype(F32), axis=0).astype(BF16)
    grads = jnp.concatenate([grads[0], swap(grads[1])], axis=1)
    copies = jnp.broadcast_to(grads[None], (8,) + grads.shape)
    grads = lax.all_to_all(copies, "z", 0, 0).reshape(128, 2048)
    low_bases = ((other_in, (extra, half)),)
    partial_acts = rotate(ring(low, "z"), "z", low_bases, here, BF16, copies, (partial_acts,))
    rot_acts = over_x(after(partial_acts, grads))
    grads = direct(grads)
    ids = lax.dynamic_index_in_dim(doc_ids.reshape(32, 2, 16), c, 1, keepdims=False)
    docs = score(grads, precond, swap(precond), rot_acts, ids, here)
    total = jnp.sum(spread(docs[:, 0, :DOCS].reshape(1, 2 * DOCS), ALL, 256), axis=0)
    return total.reshape(2, DOCS).T


def solution(mesh):
    finer = Mesh(mesh.devices.reshape(4, 8, 4, 2), ALL)
    in_specs = (
        P(WIDE, NARROW),
        P(WIDE, None),
        P(NARROW, WIDE),
        P(WIDE, NARROW),
        P(NARROW, WIDE),
        P(None, NARROW, WIDE),
        P(),
    )
    return jax.shard_map(
        shards, mesh=finer, in_specs=in_specs, out_specs=P(), check_vma=False
    )
```

```python
import functools

import jax
import jax.numpy as jnp
from jax import lax
from jax.experimental import pallas as pl
from jax.experimental.pallas import tpu as pltpu
from jax.sharding import Mesh
from jax.sharding import PartitionSpec as P

WIDE = ("y", "z")
NARROW = ("x", "c")
ALL = ("y", "z", "x", "c")
SIZE = {"y": 4, "z": 8, "x": 4, "c": 2}
DOCS = 64
DAMPING = 0.1
F32 = jnp.float32
BF16 = jnp.bfloat16
STEP = 512
SPLIT = 3584


def shift(value, axis, hops):
    size = SIZE[axis]
    return lax.ppermute(value, axis, [(i, (i + hops) % size) for i in range(size)])


def ring(chunk, axis):
    size = SIZE[axis]
    half = size // 2
    got = [(0, 0, chunk)]
    ahead = back = chunk
    for step in range(1, half):
        ahead, back = shift(ahead, axis, 1), shift(back, axis, -1)
        got += [(step, 0, ahead), (size - step, 0, back)]
    cut = chunk.shape[1] // 2
    got += [(half, 0, shift(ahead[:, :cut], axis, 1)), (half, cut, shift(back[:, cut:], axis, -1))]
    return got


def spread(value, axes, size):
    return lax.all_to_all(jnp.broadcast_to(value[None], (size,) + value.shape), axes, 0, 0)


def join_kernel(places, rows, here, *refs):
    chunks, out = refs[: len(places)], refs[-1]
    for back, chunk in zip(places, chunks):
        row = pl.multiple_of(lax.rem(here[0] + len(places) - back, len(places)) * rows, rows)
        out[pl.ds(row, rows), :] = chunk[...]


PLACES = (0, 1, 3, 2)


def direct(value):
    return [value] + [shift(value, "y", back) for back in PLACES[1:]]


def join(value, here):
    rows, cols = value.shape
    return pl.pallas_call(
        functools.partial(join_kernel, PLACES, rows),
        out_shape=jax.ShapeDtypeStruct((4 * rows, cols), BF16),
        in_specs=[pl.BlockSpec(memory_space=pltpu.SMEM)] + [pl.BlockSpec(memory_space=pltpu.VMEM)] * 4,
        out_specs=pl.BlockSpec(memory_space=pltpu.VMEM),
        cost_estimate=pl.CostEstimate(flops=0, bytes_accessed=16 * rows * cols, transcendentals=0),
        name="join",
    )(here, *direct(value))


def project_kernel(here, own, other, first, second, third, fourth, precond, out):
    for half, rows in enumerate((own, other)):
        total = 0.0
        for back, basis in zip(PLACES, (first, second, third, fourth)):
            slot = pl.multiple_of(lax.rem(here[0] + 4 - back, 4) * 256, 256)
            total += jnp.dot(rows[:, pl.ds(slot, 256)], basis[...], preferred_element_type=F32)
        out[:, half] = total.astype(BF16).reshape(8, 16, 1024)


def project(own, other, bases, precond, here):
    vmem = pl.BlockSpec(memory_space=pltpu.VMEM)
    return pl.pallas_call(
        project_kernel,
        out_shape=jax.ShapeDtypeStruct((8, 2, 16, 1024), BF16),
        in_specs=[pl.BlockSpec(memory_space=pltpu.SMEM)] + [vmem] * 6 + [pl.BlockSpec(memory_space=pl.ANY)],
        out_specs=vmem,
        cost_estimate=pl.CostEstimate(flops=2**29, bytes_accessed=2**22, transcendentals=0),
        compiler_params=pltpu.CompilerParams(vmem_limit_bytes=16 << 20),
        name="project",
    )(here, own, other, *bases, precond)


def damp_kernel(queries, eigenvalues, _, out):
    damped = eigenvalues[...].astype(F32) + DAMPING
    for q in range(2):
        out[q] = (queries[q].astype(F32) / damped).astype(BF16)


def damp(queries, eigenvalues, ready):
    count, rows, cols = queries.shape
    return pl.pallas_call(
        damp_kernel,
        grid=(rows // 128,),
        out_shape=jax.ShapeDtypeStruct((count, rows, cols), BF16),
        in_specs=[
            pl.BlockSpec((count, 128, cols), lambda i: (0, i, 0)),
            pl.BlockSpec((128, cols), lambda i: (i, 0)),
            pl.BlockSpec(memory_space=pl.ANY),
        ],
        out_specs=pl.BlockSpec((count, 128, cols), lambda i: (0, i, 0)),
        cost_estimate=pl.CostEstimate(
            flops=2 * count * rows * cols, bytes_accessed=10 * rows * cols, transcendentals=0
        ),
        compiler_params=pltpu.CompilerParams(vmem_limit_bytes=8 << 20),
        name="damp",
    )(queries, eigenvalues, ready)


def rotate_kernel(places, axis, spans, summed, here, *refs):
    count = len(places)
    chunks, bases, refs = refs[:count], refs[count : count + len(spans)], refs[count + len(spans) :]
    before, (out, lhs, rhs, total, chunk_sems, basis_sems) = refs[:summed], refs[-6:]
    steps = rhs.shape[0]
    loads = []

    for n, ((back, first, width), chunk) in enumerate(zip(places, chunks)):
        if axis == "y":
            into = lhs.at[lax.rem(here[0] + 4 - back, 4), :, :, pl.ds(first, width)]
            loads.append(pltpu.make_async_copy(chunk, into, chunk_sems.at[n]))
        else:
            loads.append(pltpu.make_async_copy(chunk.at[:, back], lhs.at[back], chunk_sems.at[n]))

    def basis_load(basis, row, k):
        return pltpu.make_async_copy(basis.at[pl.ds(row, STEP)], rhs.at[k], basis_sems.at[k])

    for n in loads:
        n.start()
    k = 0
    for basis, (first, last) in zip(bases, spans):
        for row in range(first, last, STEP):
            basis_load(basis, row, k).start()
            k += 1
    total[...] = before[0][...] if summed else jnp.zeros_like(total)
    for n in loads:
        n.wait()

    @pl.loop(0, steps)
    def _(k):
        basis_load(bases[0], 0, k).wait()
        part = lhs[:, :, :, pl.ds(pl.multiple_of(k * STEP, STEP), STEP)].reshape(512, STEP)
        total[...] += jnp.dot(part, rhs[k], preferred_element_type=F32)

    out[...] = total[...].astype(out.dtype)


def rotate(chunks, axis, bases, here, dtype, ready, before=()):
    spans = [span for _, span in bases]
    depth, cols = sum(last - first for first, last in spans), bases[0][0].shape[1]
    places = [(back, first, chunk.shape[-1]) for back, first, chunk in chunks]
    count = 512
    steps = depth // STEP
    copies = len(places)
    return pl.pallas_call(
        functools.partial(rotate_kernel, places, axis, spans, len(before)),
        out_shape=jax.ShapeDtypeStruct((count, cols), dtype),
        in_specs=[pl.BlockSpec(memory_space=pltpu.SMEM)]
        + [pl.BlockSpec(memory_space=pl.ANY)] * len(places)
        + [pl.BlockSpec(memory_space=pltpu.HBM)] * len(bases)
        + [pl.BlockSpec(memory_space=pltpu.VMEM)] * len(before)
        + [pl.BlockSpec(memory_space=pl.ANY)] * len(ready),
        out_specs=pl.BlockSpec(memory_space=pltpu.VMEM),
        scratch_shapes=[
            pltpu.VMEM((4, 8, 16, depth), BF16),
            pltpu.VMEM((steps, STEP, cols), BF16),
            pltpu.VMEM((count, cols), F32),
            pltpu.SemaphoreType.DMA((copies,)),
            pltpu.SemaphoreType.DMA((steps,)),
        ],
        cost_estimate=pl.CostEstimate(
            flops=(8 if axis == "y" else 4) * 2 * count * depth * cols,
            bytes_accessed=2 * (count * depth + depth * cols + count * cols),
            transcendentals=0,
        ),
        compiler_params=pltpu.CompilerParams(vmem_limit_bytes=48 << 20),
        name="rotate_" + axis,
    )(here, *[chunk for _, _, chunk in chunks], *[basis for basis, _ in bases], *before, *ready)


def score_kernel(grads, own, other, acts, ids, out):
    half = own.shape[1]
    mixed = jnp.dot(grads[:, :half], own[0], preferred_element_type=F32)
    mixed += jnp.dot(grads[:, half:], other[0], preferred_element_type=F32)
    token = jnp.sum(mixed * acts[...].astype(F32), axis=1, keepdims=True)
    docs = lax.broadcasted_iota(jnp.int32, (token.shape[0], 128), 1)
    out[0] = jnp.sum(jnp.where(ids[...] == docs, token, 0.0), axis=0, keepdims=True)


def score(grads, own, other, acts, ids):
    tokens, cols = acts.shape
    count, half, _ = own.shape
    return pl.pallas_call(
        score_kernel,
        grid=(count,),
        out_shape=jax.ShapeDtypeStruct((count, 1, 128), F32),
        in_specs=[
            pl.BlockSpec((tokens, 2 * half), lambda q: (0, 0)),
            pl.BlockSpec((1, half, cols), lambda q: (q, 0, 0)),
            pl.BlockSpec((1, half, cols), lambda q: (q, 0, 0)),
            pl.BlockSpec((tokens, cols), lambda q: (0, 0)),
            pl.BlockSpec((tokens, 1), lambda q: (0, 0)),
        ],
        out_specs=pl.BlockSpec((1, 1, 128), lambda q: (q, 0, 0)),
        cost_estimate=pl.CostEstimate(
            flops=4 * count * tokens * half * cols,
            bytes_accessed=2 * (2 * tokens * half + 2 * count * half * cols + tokens * cols),
            transcendentals=0,
        ),
        compiler_params=pltpu.CompilerParams(vmem_limit_bytes=24 << 20),
        name="score",
    )(grads, own, other, acts, ids.reshape(tokens, 1))


def after_kernel(value, ready, out):
    pass


def after(value, ready):
    anywhere = pl.BlockSpec(memory_space=pl.ANY)
    return pl.pallas_call(
        after_kernel,
        out_shape=jax.ShapeDtypeStruct(value.shape, value.dtype),
        in_specs=[anywhere, anywhere],
        out_specs=anywhere,
        input_output_aliases={0: 0},
        name="after",
    )(value, ready)


def over_x(partial):
    rows, cols = partial.shape
    parts = lax.all_to_all(partial.reshape(4, rows // 4, cols), "x", 0, 0)
    share = jnp.sum(parts.astype(F32), axis=0).astype(BF16)
    return spread(share, "x", 4).reshape(rows, cols)


def swap(value):
    return shift(value, "c", 1)


def shards(activations, out_grads, basis_in, basis_out, eigenvalues, queries, doc_ids):
    y, z, c = (lax.axis_index(axis) for axis in "yzc")
    here = jnp.stack([y, z])
    other_in = swap(basis_in)
    mine = lax.dynamic_slice_in_dim(activations, c * 16, 16)
    theirs = swap(lax.dynamic_slice_in_dim(activations, (1 - c) * 16, 16))
    extra = SPLIT - mine.shape[1]
    low = first_low = join(theirs[:, extra:], here)
    low = lax.all_gather(low, "z", axis=0, tiled=True).reshape(8, 4, 16, -1)
    bases = direct(after(basis_out, first_low))
    precond = damp(queries, eigenvalues, first_low)
    rows = lax.dynamic_slice_in_dim(out_grads, c * 16, 16).reshape(16, 4, 8, 256)
    rows = rows.transpose(2, 0, 1, 3).reshape(8, 16, 1024)
    mine = jnp.concatenate([mine, theirs[:, :extra]], axis=1)
    copies = jnp.broadcast_to(mine[None], (8,) + mine.shape)
    sent = lax.all_to_all(jnp.concatenate([copies, rows], axis=2), "z", 0, 0)
    high = sent[:, :, :SPLIT].reshape(128, -1)
    rows = sent[:, :, SPLIT:].reshape(128, -1)
    half = basis_in.shape[0]
    high_bases = ((basis_in, (0, half)), (other_in, (0, extra)))[: 1 + (extra > 0)]
    parts = lax.all_to_all(project(rows, swap(rows), bases, precond, here), "z", 0, 0)
    partial_acts = rotate([(back, first, chunk.reshape(8, 16, -1)) for back, first, chunk in ring(high, "y")], "y", high_bases, here, F32, (parts, low))
    grads = jnp.sum(parts.astype(F32), axis=0).astype(BF16)
    grads = jnp.concatenate([grads[0], swap(grads[1])], axis=1)
    copies = jnp.broadcast_to(grads[None], (8,) + grads.shape)
    grads = lax.all_to_all(copies, "z", 0, 0).reshape(128, 2048)
    low_bases = ((other_in, (extra, half)),)
    partial_acts = rotate([(y, 0, low) for y in range(4)], "z", low_bases, here, BF16, (copies,), (partial_acts,))
    rot_acts = over_x(after(partial_acts, grads))
    rot_grads = lax.all_gather(grads, "y", axis=0, tiled=True)
    ids = lax.dynamic_index_in_dim(doc_ids.reshape(32, 2, 16), c, 1, keepdims=False)
    docs = score(rot_grads, precond, swap(precond), rot_acts, ids)
    total = jnp.sum(spread(docs[:, 0, :DOCS].reshape(1, 2 * DOCS), ALL, 256), axis=0)
    return total.reshape(2, DOCS).T


def solution(mesh):
    finer = Mesh(mesh.devices.reshape(4, 8, 4, 2), ALL)
    in_specs = (
        P(WIDE, NARROW),
        P(WIDE, None),
        P(NARROW, WIDE),
        P(WIDE, NARROW),
        P(NARROW, WIDE),
        P(None, NARROW, WIDE),
        P(),
    )
    return jax.shard_map(
        shards, mesh=finer, in_specs=in_specs, out_specs=P(), check_vma=False
    )
```

```python
import functools

import jax
import jax.numpy as jnp
from jax import lax
from jax.experimental import pallas as pl
from jax.experimental.pallas import tpu as pltpu
from jax.sharding import Mesh
from jax.sharding import PartitionSpec as P

WIDE = ("y", "z")
NARROW = ("x", "c")
ALL = ("y", "z", "x", "c")
SIZE = {"y": 4, "z": 8, "x": 4, "c": 2}
DOCS = 64
DAMPING = 0.1
F32 = jnp.float32
BF16 = jnp.bfloat16
STEP = 512
SPLIT = 3584


def shift(value, axis, hops):
    size = SIZE[axis]
    return lax.ppermute(value, axis, [(i, (i + hops) % size) for i in range(size)])


def ring(chunk, axis):
    size = SIZE[axis]
    half = size // 2
    got = [(0, 0, chunk)]
    ahead = back = chunk
    for step in range(1, half):
        ahead, back = shift(ahead, axis, 1), shift(back, axis, -1)
        got += [(step, 0, ahead), (size - step, 0, back)]
    cut = chunk.shape[1] // 2
    got += [(half, 0, shift(ahead[:, :cut], axis, 1)), (half, cut, shift(back[:, cut:], axis, -1))]
    return got


def spread(value, axes, size):
    return lax.all_to_all(jnp.broadcast_to(value[None], (size,) + value.shape), axes, 0, 0)


def join_kernel(places, rows, here, *refs):
    chunks, out = refs[: len(places)], refs[-1]
    for back, chunk in zip(places, chunks):
        row = pl.multiple_of(lax.rem(here[0] + len(places) - back, len(places)) * rows, rows)
        out[pl.ds(row, rows), :] = chunk[...]


PLACES = (0, 1, 3, 2)


def direct(value):
    return [value] + [shift(value, "y", back) for back in PLACES[1:]]


def join(value, ready, here):
    rows, cols = value.shape
    return pl.pallas_call(
        functools.partial(join_kernel, PLACES, rows),
        out_shape=jax.ShapeDtypeStruct((4 * rows, cols), BF16),
        in_specs=[pl.BlockSpec(memory_space=pltpu.SMEM)]
        + [pl.BlockSpec(memory_space=pltpu.VMEM)] * 4
        + [pl.BlockSpec(memory_space=pl.ANY)],
        out_specs=pl.BlockSpec(memory_space=pltpu.VMEM),
        cost_estimate=pl.CostEstimate(flops=0, bytes_accessed=16 * rows * cols, transcendentals=0),
        name="join",
    )(here, *direct(value), ready)


def project_kernel(here, own, other, first, second, third, fourth, precond, out):
    for half, rows in enumerate((own, other)):
        total = 0.0
        for back, basis in zip(PLACES, (first, second, third, fourth)):
            slot = pl.multiple_of(lax.rem(here[0] + 4 - back, 4) * 256, 256)
            total += jnp.dot(rows[:, pl.ds(slot, 256)], basis[...], preferred_element_type=F32)
        out[:, half] = total.astype(BF16).reshape(8, 16, 1024)


def project(own, other, bases, precond, here):
    vmem = pl.BlockSpec(memory_space=pltpu.VMEM)
    return pl.pallas_call(
        project_kernel,
        out_shape=jax.ShapeDtypeStruct((8, 2, 16, 1024), BF16),
        in_specs=[pl.BlockSpec(memory_space=pltpu.SMEM)] + [vmem] * 6 + [pl.BlockSpec(memory_space=pl.ANY)],
        out_specs=vmem,
        cost_estimate=pl.CostEstimate(flops=2**29, bytes_accessed=2**22, transcendentals=0),
        compiler_params=pltpu.CompilerParams(vmem_limit_bytes=16 << 20),
        name="project",
    )(here, own, other, *bases, precond)


def damp_kernel(queries, eigenvalues, basis, _, out, same):
    same[...] = basis[...]
    damped = eigenvalues[...].astype(F32) + DAMPING
    for q in range(2):
        out[q] = (queries[q].astype(F32) / damped).astype(BF16)


def damp(queries, eigenvalues, basis, ready):
    count, rows, cols = queries.shape
    return pl.pallas_call(
        damp_kernel,
        grid=(rows // 128,),
        out_shape=(
            jax.ShapeDtypeStruct((count, rows, cols), BF16),
            jax.ShapeDtypeStruct(basis.shape, BF16),
        ),
        in_specs=[
            pl.BlockSpec((count, 128, cols), lambda i: (0, i, 0)),
            pl.BlockSpec((128, cols), lambda i: (i, 0)),
            pl.BlockSpec((32, basis.shape[1]), lambda i: (i, 0)),
            pl.BlockSpec(memory_space=pl.ANY),
        ],
        out_specs=(
            pl.BlockSpec((count, 128, cols), lambda i: (0, i, 0)),
            pl.BlockSpec((32, basis.shape[1]), lambda i: (i, 0)),
        ),
        cost_estimate=pl.CostEstimate(
            flops=2 * count * rows * cols, bytes_accessed=10 * rows * cols, transcendentals=0
        ),
        compiler_params=pltpu.CompilerParams(vmem_limit_bytes=56 << 20),
        name="damp",
    )(queries, eigenvalues, basis, ready)


def rotate_kernel(places, axis, spans, summed, here, *refs):
    count = len(places)
    chunks, bases, refs = refs[:count], refs[count : count + len(spans)], refs[count + len(spans) :]
    before, (out, lhs, rhs, total, chunk_sems, basis_sems) = refs[:summed], refs[-6:]
    steps = rhs.shape[0]
    loads = []

    for n, ((back, first, width), chunk) in enumerate(zip(places, chunks)):
        if axis == "y":
            into = lhs.at[lax.rem(here[0] + 4 - back, 4), :, :, pl.ds(first, width)]
            loads.append(pltpu.make_async_copy(chunk, into, chunk_sems.at[n]))
        else:
            loads.append(pltpu.make_async_copy(chunk.at[:, back], lhs.at[back], chunk_sems.at[n]))

    def basis_load(basis, row, k):
        return pltpu.make_async_copy(basis.at[pl.ds(row, STEP)], rhs.at[k], basis_sems.at[k])

    for n in loads:
        n.start()
    k = 0
    for basis, (first, last) in zip(bases, spans):
        for row in range(first, last, STEP):
            basis_load(basis, row, k).start()
            k += 1
    total[...] = before[0][...] if summed else jnp.zeros_like(total)
    for n in loads:
        n.wait()

    @pl.loop(0, steps)
    def _(k):
        basis_load(bases[0], 0, k).wait()
        part = lhs[:, :, :, pl.ds(pl.multiple_of(k * STEP, STEP), STEP)].reshape(512, STEP)
        total[...] += jnp.dot(part, rhs[k], preferred_element_type=F32)

    out[...] = total[...].astype(out.dtype)


def rotate(chunks, axis, bases, here, dtype, ready, before=()):
    spans = [span for _, span in bases]
    depth, cols = sum(last - first for first, last in spans), bases[0][0].shape[1]
    places = [(back, first, chunk.shape[-1]) for back, first, chunk in chunks]
    count = 512
    steps = depth // STEP
    copies = len(places)
    return pl.pallas_call(
        functools.partial(rotate_kernel, places, axis, spans, len(before)),
        out_shape=jax.ShapeDtypeStruct((count, cols), dtype),
        in_specs=[pl.BlockSpec(memory_space=pltpu.SMEM)]
        + [pl.BlockSpec(memory_space=pl.ANY)] * len(places)
        + [pl.BlockSpec(memory_space=pltpu.HBM)] * len(bases)
        + [pl.BlockSpec(memory_space=pltpu.VMEM)] * len(before)
        + [pl.BlockSpec(memory_space=pl.ANY)] * len(ready),
        out_specs=pl.BlockSpec(memory_space=pltpu.VMEM),
        scratch_shapes=[
            pltpu.VMEM((4, 8, 16, depth), BF16),
            pltpu.VMEM((steps, STEP, cols), BF16),
            pltpu.VMEM((count, cols), F32),
            pltpu.SemaphoreType.DMA((copies,)),
            pltpu.SemaphoreType.DMA((steps,)),
        ],
        cost_estimate=pl.CostEstimate(
            flops=(4 if axis == "y" else 4) * 2 * count * depth * cols,
            bytes_accessed=2 * (count * depth + depth * cols + count * cols),
            transcendentals=0,
        ),
        compiler_params=pltpu.CompilerParams(vmem_limit_bytes=48 << 20),
        name="rotate_" + axis,
    )(here, *[chunk for _, _, chunk in chunks], *[basis for basis, _ in bases], *before, *ready)


def score_kernel(grads, own, other, acts, ids, out):
    half = own.shape[1]
    mixed = jnp.dot(grads[:, :half], own[0], preferred_element_type=F32)
    mixed += jnp.dot(grads[:, half:], other[0], preferred_element_type=F32)
    token = jnp.sum(mixed * acts[...].astype(F32), axis=1, keepdims=True)
    docs = lax.broadcasted_iota(jnp.int32, (token.shape[0], 128), 1)
    out[0] = jnp.sum(jnp.where(ids[...] == docs, token, 0.0), axis=0, keepdims=True)


def score(grads, own, other, acts, ids):
    tokens, cols = acts.shape
    count, half, _ = own.shape
    return pl.pallas_call(
        score_kernel,
        grid=(count,),
        out_shape=jax.ShapeDtypeStruct((count, 1, 128), F32),
        in_specs=[
            pl.BlockSpec((tokens, 2 * half), lambda q: (0, 0)),
            pl.BlockSpec((1, half, cols), lambda q: (q, 0, 0)),
            pl.BlockSpec((1, half, cols), lambda q: (q, 0, 0)),
            pl.BlockSpec((tokens, cols), lambda q: (0, 0)),
            pl.BlockSpec((tokens, 1), lambda q: (0, 0)),
        ],
        out_specs=pl.BlockSpec((1, 1, 128), lambda q: (q, 0, 0)),
        cost_estimate=pl.CostEstimate(
            flops=4 * count * tokens * half * cols,
            bytes_accessed=2 * (2 * tokens * half + 2 * count * half * cols + tokens * cols),
            transcendentals=0,
        ),
        compiler_params=pltpu.CompilerParams(vmem_limit_bytes=56 << 20),
        name="score",
    )(grads, own, other, acts, ids.reshape(tokens, 1))


def after_kernel(value, ready, out):
    pass


def after(value, ready):
    anywhere = pl.BlockSpec(memory_space=pl.ANY)
    return pl.pallas_call(
        after_kernel,
        out_shape=jax.ShapeDtypeStruct(value.shape, value.dtype),
        in_specs=[anywhere, anywhere],
        out_specs=anywhere,
        input_output_aliases={0: 0},
        name="after",
    )(value, ready)


def over_x(partial):
    rows, cols = partial.shape
    parts = lax.all_to_all(partial.reshape(4, rows // 4, cols), "x", 0, 0)
    share = jnp.sum(parts.astype(F32), axis=0).astype(BF16)
    return spread(share, "x", 4).reshape(rows, cols)


def swap(value):
    return shift(value, "c", 1)


def shards(activations, out_grads, basis_in, basis_out, eigenvalues, queries, doc_ids):
    y, z, c = (lax.axis_index(axis) for axis in "yzc")
    here = jnp.stack([y, z])
    other_in = swap(basis_in)
    mine = lax.dynamic_slice_in_dim(activations, c * 16, 16)
    theirs = swap(lax.dynamic_slice_in_dim(activations, (1 - c) * 16, 16))
    extra = SPLIT - mine.shape[1]
    rows = lax.dynamic_slice_in_dim(out_grads, c * 16, 16).reshape(16, 4, 8, 256)
    rows = rows.transpose(2, 0, 1, 3).reshape(8, 16, 1024)
    rows = lax.all_to_all(rows, "z", 0, 0).reshape(128, -1)
    low = first_low = join(theirs[:, extra:], rows, here)
    low = lax.all_gather(low, "z", axis=0, tiled=True).reshape(8, 4, 16, -1)
    precond, basis_out = damp(queries, eigenvalues, basis_out, first_low)
    bases = direct(basis_out)
    mine = jnp.concatenate([mine, theirs[:, :extra]], axis=1)
    high = spread(mine, "z", 8).reshape(128, -1)
    half = basis_in.shape[0]
    high_bases = ((basis_in, (0, half)), (other_in, (0, extra)))[: 1 + (extra > 0)]
    parts = lax.all_to_all(project(rows, swap(rows), bases, precond, here), "z", 0, 0)
    partial_acts = rotate([(back, first, chunk.reshape(8, 16, -1)) for back, first, chunk in ring(high, "y")], "y", high_bases, here, F32, (parts, low))
    grads = jnp.sum(parts.astype(F32), axis=0).astype(BF16)
    grads = jnp.concatenate([grads[0], swap(grads[1])], axis=1)
    copies = jnp.broadcast_to(grads[None], (8,) + grads.shape)
    grads = lax.all_to_all(copies, "z", 0, 0).reshape(128, 2048)
    low_bases = ((other_in, (extra, half)),)
    partial_acts = rotate([(y, 0, low) for y in range(4)], "z", low_bases, here, BF16, (copies,), (partial_acts,))
    rot_acts = over_x(after(partial_acts, grads))
    rot_grads = lax.all_gather(grads, "y", axis=0, tiled=True)
    ids = lax.dynamic_index_in_dim(doc_ids.reshape(32, 2, 16), c, 1, keepdims=False)
    docs = score(rot_grads, precond, swap(precond), rot_acts, ids)
    total = jnp.sum(spread(docs[:, 0, :DOCS].reshape(1, 2 * DOCS), ALL, 256), axis=0)
    return total.reshape(2, DOCS).T


def solution(mesh):
    finer = Mesh(mesh.devices.reshape(4, 8, 4, 2), ALL)
    in_specs = (
        P(WIDE, NARROW),
        P(WIDE, None),
        P(NARROW, WIDE),
        P(WIDE, NARROW),
        P(NARROW, WIDE),
        P(None, NARROW, WIDE),
        P(),
    )
    return jax.shard_map(
        shards, mesh=finer, in_specs=in_specs, out_specs=P(), check_vma=False
    )
```

```python
import functools

import jax
import jax.numpy as jnp
from jax import lax
from jax.experimental import pallas as pl
from jax.experimental.pallas import tpu as pltpu
from jax.sharding import Mesh
from jax.sharding import PartitionSpec as P

WIDE = ("y", "z")
NARROW = ("x", "c")
ALL = ("y", "z", "x", "c")
SIZE = {"y": 4, "z": 8, "x": 4, "c": 2}
DOCS = 64
DAMPING = 0.1
F32 = jnp.float32
BF16 = jnp.bfloat16
STEP = 512
SPLIT = 3584


def shift(value, axis, hops):
    size = SIZE[axis]
    return lax.ppermute(value, axis, [(i, (i + hops) % size) for i in range(size)])


def ring(chunk, axis):
    size = SIZE[axis]
    half = size // 2
    got = [(0, 0, chunk)]
    ahead = back = chunk
    for step in range(1, half):
        ahead, back = shift(ahead, axis, 1), shift(back, axis, -1)
        got += [(step, 0, ahead), (size - step, 0, back)]
    cut = chunk.shape[1] // 2
    got += [(half, 0, shift(ahead[:, :cut], axis, 1)), (half, cut, shift(back[:, cut:], axis, -1))]
    return got


def spread(value, axes, size):
    return lax.all_to_all(jnp.broadcast_to(value[None], (size,) + value.shape), axes, 0, 0)


def join_kernel(places, rows, here, *refs):
    chunks, (basis, out, same) = refs[: len(places)], refs[len(places) :]
    same[...] = basis[...]
    for back, chunk in zip(places, chunks):
        row = pl.multiple_of(lax.rem(here[0] + len(places) - back, len(places)) * rows, rows)
        out[pl.ds(row, rows), :] = chunk[...]


PLACES = (0, 1, 3, 2)


def direct(value):
    return [value] + [shift(value, "y", back) for back in PLACES[1:]]


def join(value, basis, here):
    rows, cols = value.shape
    return pl.pallas_call(
        functools.partial(join_kernel, PLACES, rows),
        out_shape=(jax.ShapeDtypeStruct((4 * rows, cols), BF16), jax.ShapeDtypeStruct(basis.shape, BF16)),
        in_specs=[pl.BlockSpec(memory_space=pltpu.SMEM)] + [pl.BlockSpec(memory_space=pltpu.VMEM)] * 5,
        out_specs=(pl.BlockSpec(memory_space=pltpu.VMEM), pl.BlockSpec(memory_space=pltpu.VMEM)),
        cost_estimate=pl.CostEstimate(flops=0, bytes_accessed=16 * rows * cols, transcendentals=0),
        name="join",
    )(here, *direct(value), basis)


def project_kernel(here, own, other, first, second, third, left, right, out):
    for half, rows in enumerate((own, other)):
        total = 0.0
        for back, parts in ((0, (first,)), (1, (second,)), (3, (third,)), (2, (left, right))):
            slot = pl.multiple_of(lax.rem(here[0] + 4 - back, 4) * 256, 256)
            part = rows[:, pl.ds(slot, 256)]
            sums = [jnp.dot(part, basis[...], preferred_element_type=F32) for basis in parts]
            total += sums[0] if len(sums) == 1 else jnp.concatenate(sums, axis=1)
        out[:, half] = total.astype(BF16).reshape(8, 16, 1024)


def project(own, other, bases, here):
    vmem = pl.BlockSpec(memory_space=pltpu.VMEM)
    return pl.pallas_call(
        project_kernel,
        out_shape=jax.ShapeDtypeStruct((8, 2, 16, 1024), BF16),
        in_specs=[pl.BlockSpec(memory_space=pltpu.SMEM)] + [vmem] * 7,
        out_specs=vmem,
        cost_estimate=pl.CostEstimate(flops=50 * 2**29, bytes_accessed=2**22, transcendentals=0),
        compiler_params=pltpu.CompilerParams(vmem_limit_bytes=16 << 20),
        name="project",
    )(here, own, other, *bases)


def damp_kernel(queries, eigenvalues, _, out):
    damped = eigenvalues[...].astype(F32) + DAMPING
    for q in range(2):
        out[q] = (queries[q].astype(F32) / damped).astype(BF16)


def damp(queries, eigenvalues, ready):
    count, rows, cols = queries.shape
    return pl.pallas_call(
        damp_kernel,
        grid=(rows // 128,),
        out_shape=jax.ShapeDtypeStruct((count, rows, cols), BF16),
        in_specs=[
            pl.BlockSpec((count, 128, cols), lambda i: (0, i, 0)),
            pl.BlockSpec((128, cols), lambda i: (i, 0)),
            pl.BlockSpec(memory_space=pl.ANY),
        ],
        out_specs=pl.BlockSpec((count, 128, cols), lambda i: (0, i, 0)),
        cost_estimate=pl.CostEstimate(
            flops=2 * count * rows * cols, bytes_accessed=10 * rows * cols, transcendentals=0
        ),
        compiler_params=pltpu.CompilerParams(vmem_limit_bytes=56 << 20),
        name="damp",
    )(queries, eigenvalues, ready)


def rotate_kernel(places, axis, spans, summed, here, *refs):
    count = len(places)
    chunks, bases, refs = refs[:count], refs[count : count + len(spans)], refs[count + len(spans) :]
    before, (out, lhs, rhs, total, chunk_sems, basis_sems) = refs[:summed], refs[-6:]
    steps = rhs.shape[0]
    loads = []

    for n, ((back, first, width), chunk) in enumerate(zip(places, chunks)):
        if axis == "y":
            into = lhs.at[lax.rem(here[0] + 4 - back, 4), :, :, pl.ds(first, width)]
            loads.append(pltpu.make_async_copy(chunk, into, chunk_sems.at[n]))
        else:
            loads.append(pltpu.make_async_copy(chunk.at[:, back], lhs.at[back], chunk_sems.at[n]))

    def basis_load(basis, row, k):
        return pltpu.make_async_copy(basis.at[pl.ds(row, STEP)], rhs.at[k], basis_sems.at[k])

    for n in loads:
        n.start()
    k = 0
    for basis, (first, last) in zip(bases, spans):
        for row in range(first, last, STEP):
            basis_load(basis, row, k).start()
            k += 1
    total[...] = before[0][...] if summed else jnp.zeros_like(total)
    for n in loads:
        n.wait()

    @pl.loop(0, steps)
    def _(k):
        basis_load(bases[0], 0, k).wait()
        part = lhs[:, :, :, pl.ds(pl.multiple_of(k * STEP, STEP), STEP)].reshape(512, STEP)
        total[...] += jnp.dot(part, rhs[k], preferred_element_type=F32)

    out[...] = total[...].astype(out.dtype)


def rotate(chunks, axis, bases, here, dtype, ready, before=()):
    spans = [span for _, span in bases]
    depth, cols = sum(last - first for first, last in spans), bases[0][0].shape[1]
    places = [(back, first, chunk.shape[-1]) for back, first, chunk in chunks]
    count = 512
    steps = depth // STEP
    copies = len(places)
    return pl.pallas_call(
        functools.partial(rotate_kernel, places, axis, spans, len(before)),
        out_shape=jax.ShapeDtypeStruct((count, cols), dtype),
        in_specs=[pl.BlockSpec(memory_space=pltpu.SMEM)]
        + [pl.BlockSpec(memory_space=pl.ANY)] * len(places)
        + [pl.BlockSpec(memory_space=pltpu.HBM)] * len(bases)
        + [pl.BlockSpec(memory_space=pltpu.VMEM)] * len(before)
        + [pl.BlockSpec(memory_space=pl.ANY)] * len(ready),
        out_specs=pl.BlockSpec(memory_space=pltpu.VMEM),
        scratch_shapes=[
            pltpu.VMEM((4, 8, 16, depth), BF16),
            pltpu.VMEM((steps, STEP, cols), BF16),
            pltpu.VMEM((count, cols), F32),
            pltpu.SemaphoreType.DMA((copies,)),
            pltpu.SemaphoreType.DMA((steps,)),
        ],
        cost_estimate=pl.CostEstimate(
            flops=(4 if axis == "y" else 4) * 2 * count * depth * cols,
            bytes_accessed=2 * (count * depth + depth * cols + count * cols),
            transcendentals=0,
        ),
        compiler_params=pltpu.CompilerParams(vmem_limit_bytes=48 << 20),
        name="rotate_" + axis,
    )(here, *[chunk for _, _, chunk in chunks], *[basis for basis, _ in bases], *before, *ready)


def score_kernel(grads, own, other, acts, ids, out):
    half = own.shape[1]
    mixed = jnp.dot(grads[:, :half], own[0], preferred_element_type=F32)
    mixed += jnp.dot(grads[:, half:], other[0], preferred_element_type=F32)
    token = jnp.sum(mixed * acts[...].astype(F32), axis=1, keepdims=True)
    docs = lax.broadcasted_iota(jnp.int32, (token.shape[0], 128), 1)
    out[0] = jnp.sum(jnp.where(ids[...] == docs, token, 0.0), axis=0, keepdims=True)


def score(grads, own, other, acts, ids):
    tokens, cols = acts.shape
    count, half, _ = own.shape
    return pl.pallas_call(
        score_kernel,
        grid=(count,),
        out_shape=jax.ShapeDtypeStruct((count, 1, 128), F32),
        in_specs=[
            pl.BlockSpec((tokens, 2 * half), lambda q: (0, 0)),
            pl.BlockSpec((1, half, cols), lambda q: (q, 0, 0)),
            pl.BlockSpec((1, half, cols), lambda q: (q, 0, 0)),
            pl.BlockSpec((tokens, cols), lambda q: (0, 0)),
            pl.BlockSpec((tokens, 1), lambda q: (0, 0)),
        ],
        out_specs=pl.BlockSpec((1, 1, 128), lambda q: (q, 0, 0)),
        cost_estimate=pl.CostEstimate(
            flops=4 * count * tokens * half * cols,
            bytes_accessed=2 * (2 * tokens * half + 2 * count * half * cols + tokens * cols),
            transcendentals=0,
        ),
        compiler_params=pltpu.CompilerParams(vmem_limit_bytes=56 << 20),
        name="score",
    )(grads, own, other, acts, ids.reshape(tokens, 1))


def after_kernel(value, ready, out):
    pass


def after(value, ready):
    anywhere = pl.BlockSpec(memory_space=pl.ANY)
    return pl.pallas_call(
        after_kernel,
        out_shape=jax.ShapeDtypeStruct(value.shape, value.dtype),
        in_specs=[anywhere, anywhere],
        out_specs=anywhere,
        input_output_aliases={0: 0},
        name="after",
    )(value, ready)


def over_x(partial):
    rows, cols = partial.shape
    parts = lax.all_to_all(partial.reshape(4, rows // 4, cols), "x", 0, 0)
    share = jnp.sum(parts.astype(F32), axis=0).astype(BF16)
    return spread(share, "x", 4).reshape(rows, cols)


def swap(value):
    return shift(value, "c", 1)


def shards(activations, out_grads, basis_in, basis_out, eigenvalues, queries, doc_ids):
    y, z, c = (lax.axis_index(axis) for axis in "yzc")
    here = jnp.stack([y, z])
    other_in = swap(basis_in)
    mine = lax.dynamic_slice_in_dim(activations, c * 16, 16)
    theirs = swap(lax.dynamic_slice_in_dim(activations, (1 - c) * 16, 16))
    extra = SPLIT - mine.shape[1]
    first_low, basis_out = join(theirs[:, extra:], basis_out, here)
    low = first_low
    low = lax.all_gather(low, "z", axis=0, tiled=True).reshape(8, 4, 16, -1)
    cut = basis_out.shape[1] // 2
    bases = [basis_out, shift(basis_out, "y", 1), shift(basis_out, "y", -1)]
    bases += [shift(basis_out[:, :cut], "y", 2), shift(basis_out[:, cut:], "y", -2)]
    precond = damp(queries, eigenvalues, first_low)
    rows = lax.dynamic_slice_in_dim(out_grads, c * 16, 16).reshape(16, 4, 8, 256)
    rows = rows.transpose(2, 0, 1, 3).reshape(8, 16, 1024)
    mine = jnp.concatenate([mine, theirs[:, :extra]], axis=1)
    copies = jnp.broadcast_to(mine[None], (8,) + mine.shape)
    sent = lax.all_to_all(jnp.concatenate([copies, rows], axis=2), "z", 0, 0)
    high = sent[:, :, :SPLIT].reshape(128, -1)
    rows = sent[:, :, SPLIT:].reshape(128, -1)
    half = basis_in.shape[0]
    high_bases = ((basis_in, (0, half)), (other_in, (0, extra)))[: 1 + (extra > 0)]
    parts = lax.all_to_all(project(rows, swap(rows), bases, here), "z", 0, 0)
    partial_acts = rotate([(back, first, chunk.reshape(8, 16, -1)) for back, first, chunk in ring(high, "y")], "y", high_bases, here, F32, (parts, low))
    grads = jnp.sum(parts.astype(F32), axis=0).astype(BF16)
    grads = jnp.concatenate([grads[0], swap(grads[1])], axis=1)
    copies = jnp.broadcast_to(grads[None], (8,) + grads.shape)
    grads = lax.all_to_all(copies, "z", 0, 0).reshape(128, 2048)
    low_bases = ((other_in, (extra, half)),)
    partial_acts = rotate([(y, 0, low) for y in range(4)], "z", low_bases, here, BF16, (copies,), (partial_acts,))
    rot_acts = over_x(after(partial_acts, grads))
    rot_grads = lax.all_gather(grads, "y", axis=0, tiled=True)
    ids = lax.dynamic_index_in_dim(doc_ids.reshape(32, 2, 16), c, 1, keepdims=False)
    docs = score(rot_grads, precond, swap(precond), rot_acts, ids)
    total = jnp.sum(spread(docs[:, 0, :DOCS].reshape(1, 2 * DOCS), ALL, 256), axis=0)
    return total.reshape(2, DOCS).T


def solution(mesh):
    finer = Mesh(mesh.devices.reshape(4, 8, 4, 2), ALL)
    in_specs = (
        P(WIDE, NARROW),
        P(WIDE, None),
        P(NARROW, WIDE),
        P(WIDE, NARROW),
        P(NARROW, WIDE),
        P(None, NARROW, WIDE),
        P(),
    )
    return jax.shard_map(
        shards, mesh=finer, in_specs=in_specs, out_specs=P(), check_vma=False
    )
```

```python
import functools

import jax
import jax.numpy as jnp
from jax import lax
from jax.experimental import pallas as pl
from jax.experimental.pallas import tpu as pltpu
from jax.sharding import Mesh
from jax.sharding import PartitionSpec as P

WIDE = ("y", "z")
NARROW = ("x", "c")
ALL = ("y", "z", "x", "c")
SIZE = {"y": 4, "z": 8, "x": 4, "c": 2}
DOCS = 64
DAMPING = 0.1
F32 = jnp.float32
BF16 = jnp.bfloat16
STEP = 512
SPLIT = 3584


def shift(value, axis, hops):
    size = SIZE[axis]
    return lax.ppermute(value, axis, [(i, (i + hops) % size) for i in range(size)])


def ring(chunk, axis):
    size = SIZE[axis]
    half = size // 2
    got = [(0, 0, chunk)]
    ahead = back = chunk
    for step in range(1, half):
        ahead, back = shift(ahead, axis, 1), shift(back, axis, -1)
        got += [(step, 0, ahead), (size - step, 0, back)]
    cut = chunk.shape[1] // 2
    got += [(half, 0, shift(ahead[:, :cut], axis, 1)), (half, cut, shift(back[:, cut:], axis, -1))]
    return got


def spread(value, axes, size):
    return lax.all_to_all(jnp.broadcast_to(value[None], (size,) + value.shape), axes, 0, 0)


def join_kernel(places, rows, here, *refs):
    chunks, (basis, out, same) = refs[: len(places)], refs[len(places) :]
    same[...] = basis[...]
    for back, chunk in zip(places, chunks):
        row = pl.multiple_of(lax.rem(here[0] + len(places) - back, len(places)) * rows, rows)
        out[pl.ds(row, rows), :] = chunk[...]


PLACES = (0, 1, 3, 2)


def direct(value):
    return [value] + [shift(value, "y", back) for back in PLACES[1:]]


def join(value, basis, here):
    rows, cols = value.shape
    return pl.pallas_call(
        functools.partial(join_kernel, PLACES, rows),
        out_shape=(jax.ShapeDtypeStruct((4 * rows, cols), BF16), jax.ShapeDtypeStruct(basis.shape, BF16)),
        in_specs=[pl.BlockSpec(memory_space=pltpu.SMEM)] + [pl.BlockSpec(memory_space=pltpu.VMEM)] * 5,
        out_specs=(pl.BlockSpec(memory_space=pltpu.VMEM), pl.BlockSpec(memory_space=pltpu.VMEM)),
        cost_estimate=pl.CostEstimate(flops=0, bytes_accessed=16 * rows * cols, transcendentals=0),
        name="join",
    )(here, *direct(value), basis)


def project_kernel(here, own, other, first, second, third, left, right, out):
    for half, rows in enumerate((own, other)):
        total = 0.0
        for back, parts in ((0, (first,)), (1, (second,)), (3, (third,)), (2, (left, right))):
            slot = pl.multiple_of(lax.rem(here[0] + 4 - back, 4) * 256, 256)
            part = rows[:, pl.ds(slot, 256)]
            sums = [jnp.dot(part, basis[...], preferred_element_type=F32) for basis in parts]
            total += sums[0] if len(sums) == 1 else jnp.concatenate(sums, axis=1)
        out[:, half] = total.astype(BF16).reshape(8, 16, 1024)


def project(own, other, bases, here):
    vmem = pl.BlockSpec(memory_space=pltpu.VMEM)
    return pl.pallas_call(
        project_kernel,
        out_shape=jax.ShapeDtypeStruct((8, 2, 16, 1024), BF16),
        in_specs=[pl.BlockSpec(memory_space=pltpu.SMEM)] + [vmem] * 7,
        out_specs=vmem,
        cost_estimate=pl.CostEstimate(flops=75 * 2**29, bytes_accessed=2**22, transcendentals=0),
        compiler_params=pltpu.CompilerParams(vmem_limit_bytes=16 << 20),
        name="project",
    )(here, own, other, *bases)


def damp_kernel(queries, eigenvalues, _, out):
    damped = eigenvalues[...].astype(F32) + DAMPING
    for q in range(2):
        out[q] = (queries[q].astype(F32) / damped).astype(BF16)


def damp(queries, eigenvalues, ready):
    count, rows, cols = queries.shape
    return pl.pallas_call(
        damp_kernel,
        grid=(rows // 128,),
        out_shape=jax.ShapeDtypeStruct((count, rows, cols), BF16),
        in_specs=[
            pl.BlockSpec((count, 128, cols), lambda i: (0, i, 0)),
            pl.BlockSpec((128, cols), lambda i: (i, 0)),
            pl.BlockSpec(memory_space=pl.ANY),
        ],
        out_specs=pl.BlockSpec((count, 128, cols), lambda i: (0, i, 0)),
        cost_estimate=pl.CostEstimate(
            flops=2 * count * rows * cols, bytes_accessed=10 * rows * cols, transcendentals=0
        ),
        compiler_params=pltpu.CompilerParams(vmem_limit_bytes=56 << 20),
        name="damp",
    )(queries, eigenvalues, ready)


def rotate_kernel(places, axis, spans, summed, here, *refs):
    count = len(places)
    chunks, bases, refs = refs[:count], refs[count : count + len(spans)], refs[count + len(spans) :]
    before, (out, lhs, rhs, total, chunk_sems, basis_sems) = refs[:summed], refs[-6:]
    steps = rhs.shape[0]
    loads = []

    for n, ((back, first, width), chunk) in enumerate(zip(places, chunks)):
        if axis == "y":
            into = lhs.at[lax.rem(here[0] + 4 - back, 4), :, :, pl.ds(first, width)]
            loads.append(pltpu.make_async_copy(chunk, into, chunk_sems.at[n]))
        else:
            loads.append(pltpu.make_async_copy(chunk.at[:, back], lhs.at[back], chunk_sems.at[n]))

    def basis_load(basis, row, k):
        return pltpu.make_async_copy(basis.at[pl.ds(row, STEP)], rhs.at[k], basis_sems.at[k])

    for n in loads:
        n.start()
    k = 0
    for basis, (first, last) in zip(bases, spans):
        for row in range(first, last, STEP):
            basis_load(basis, row, k).start()
            k += 1
    total[...] = before[0][...] if summed else jnp.zeros_like(total)
    for n in loads:
        n.wait()

    @pl.loop(0, steps)
    def _(k):
        basis_load(bases[0], 0, k).wait()
        part = lhs[:, :, :, pl.ds(pl.multiple_of(k * STEP, STEP), STEP)].reshape(512, STEP)
        total[...] += jnp.dot(part, rhs[k], preferred_element_type=F32)

    out[...] = total[...].astype(out.dtype)


def rotate(chunks, axis, bases, here, dtype, ready, before=()):
    spans = [span for _, span in bases]
    depth, cols = sum(last - first for first, last in spans), bases[0][0].shape[1]
    places = [(back, first, chunk.shape[-1]) for back, first, chunk in chunks]
    count = 512
    steps = depth // STEP
    copies = len(places)
    return pl.pallas_call(
        functools.partial(rotate_kernel, places, axis, spans, len(before)),
        out_shape=jax.ShapeDtypeStruct((count, cols), dtype),
        in_specs=[pl.BlockSpec(memory_space=pltpu.SMEM)]
        + [pl.BlockSpec(memory_space=pl.ANY)] * len(places)
        + [pl.BlockSpec(memory_space=pltpu.HBM)] * len(bases)
        + [pl.BlockSpec(memory_space=pltpu.VMEM)] * len(before)
        + [pl.BlockSpec(memory_space=pl.ANY)] * len(ready),
        out_specs=pl.BlockSpec(memory_space=pltpu.VMEM),
        scratch_shapes=[
            pltpu.VMEM((4, 8, 16, depth), BF16),
            pltpu.VMEM((steps, STEP, cols), BF16),
            pltpu.VMEM((count, cols), F32),
            pltpu.SemaphoreType.DMA((copies,)),
            pltpu.SemaphoreType.DMA((steps,)),
        ],
        cost_estimate=pl.CostEstimate(
            flops=(4 if axis == "y" else 4) * 2 * count * depth * cols,
            bytes_accessed=2 * (count * depth + depth * cols + count * cols),
            transcendentals=0,
        ),
        compiler_params=pltpu.CompilerParams(vmem_limit_bytes=48 << 20),
        name="rotate_" + axis,
    )(here, *[chunk for _, _, chunk in chunks], *[basis for basis, _ in bases], *before, *ready)


def score_kernel(grads, own, other, acts, ids, out):
    half = own.shape[1]
    mixed = jnp.dot(grads[:, :half], own[0], preferred_element_type=F32)
    mixed += jnp.dot(grads[:, half:], other[0], preferred_element_type=F32)
    token = jnp.sum(mixed * acts[...].astype(F32), axis=1, keepdims=True)
    docs = lax.broadcasted_iota(jnp.int32, (token.shape[0], 128), 1)
    out[0] = jnp.sum(jnp.where(ids[...] == docs, token, 0.0), axis=0, keepdims=True)


def score(grads, own, other, acts, ids):
    tokens, cols = acts.shape
    count, half, _ = own.shape
    return pl.pallas_call(
        score_kernel,
        grid=(count,),
        out_shape=jax.ShapeDtypeStruct((count, 1, 128), F32),
        in_specs=[
            pl.BlockSpec((tokens, 2 * half), lambda q: (0, 0)),
            pl.BlockSpec((1, half, cols), lambda q: (q, 0, 0)),
            pl.BlockSpec((1, half, cols), lambda q: (q, 0, 0)),
            pl.BlockSpec((tokens, cols), lambda q: (0, 0)),
            pl.BlockSpec((tokens, 1), lambda q: (0, 0)),
        ],
        out_specs=pl.BlockSpec((1, 1, 128), lambda q: (q, 0, 0)),
        cost_estimate=pl.CostEstimate(
            flops=4 * count * tokens * half * cols,
            bytes_accessed=2 * (2 * tokens * half + 2 * count * half * cols + tokens * cols),
            transcendentals=0,
        ),
        compiler_params=pltpu.CompilerParams(vmem_limit_bytes=56 << 20),
        name="score",
    )(grads, own, other, acts, ids.reshape(tokens, 1))


def after_kernel(value, ready, out):
    pass


def after(value, ready):
    anywhere = pl.BlockSpec(memory_space=pl.ANY)
    return pl.pallas_call(
        after_kernel,
        out_shape=jax.ShapeDtypeStruct(value.shape, value.dtype),
        in_specs=[anywhere, anywhere],
        out_specs=anywhere,
        input_output_aliases={0: 0},
        name="after",
    )(value, ready)


def over_x(partial):
    rows, cols = partial.shape
    parts = lax.all_to_all(partial.reshape(4, rows // 4, cols), "x", 0, 0)
    share = jnp.sum(parts.astype(F32), axis=0).astype(BF16)
    return spread(share, "x", 4).reshape(rows, cols)


def swap(value):
    return shift(value, "c", 1)


def shards(activations, out_grads, basis_in, basis_out, eigenvalues, queries, doc_ids):
    y, z, c = (lax.axis_index(axis) for axis in "yzc")
    here = jnp.stack([y, z])
    other_in = swap(basis_in)
    mine = lax.dynamic_slice_in_dim(activations, c * 16, 16)
    theirs = swap(lax.dynamic_slice_in_dim(activations, (1 - c) * 16, 16))
    extra = SPLIT - mine.shape[1]
    first_low, basis_out = join(theirs[:, extra:], basis_out, here)
    low = first_low
    low = lax.all_gather(low, "z", axis=0, tiled=True).reshape(8, 4, 16, -1)
    cut = basis_out.shape[1] // 2
    bases = [basis_out, shift(basis_out, "y", 1), shift(basis_out, "y", -1)]
    bases += [shift(basis_out[:, :cut], "y", 2), shift(basis_out[:, cut:], "y", -2)]
    precond = damp(queries, eigenvalues, first_low)
    rows = lax.dynamic_slice_in_dim(out_grads, c * 16, 16).reshape(16, 4, 8, 256)
    rows = rows.transpose(2, 0, 1, 3).reshape(8, 16, 1024)
    mine = jnp.concatenate([mine, theirs[:, :extra]], axis=1)
    copies = jnp.broadcast_to(mine[None], (8,) + mine.shape)
    sent = lax.all_to_all(jnp.concatenate([copies, rows], axis=2), "z", 0, 0)
    high = sent[:, :, :SPLIT].reshape(128, -1)
    rows = sent[:, :, SPLIT:].reshape(128, -1)
    half = basis_in.shape[0]
    high_bases = ((basis_in, (0, half)), (other_in, (0, extra)))[: 1 + (extra > 0)]
    parts = lax.all_to_all(project(rows, swap(rows), bases, here), "z", 0, 0)
    partial_acts = rotate([(back, first, chunk.reshape(8, 16, -1)) for back, first, chunk in ring(high, "y")], "y", high_bases, here, F32, (parts, low))
    grads = jnp.sum(parts.astype(F32), axis=0).astype(BF16)
    grads = jnp.concatenate([grads[0], swap(grads[1])], axis=1)
    copies = jnp.broadcast_to(grads[None], (8,) + grads.shape)
    grads = lax.all_to_all(copies, "z", 0, 0).reshape(128, 2048)
    low_bases = ((other_in, (extra, half)),)
    partial_acts = rotate([(y, 0, low) for y in range(4)], "z", low_bases, here, BF16, (copies,), (partial_acts,))
    grads = after(grads, partial_acts)
    rot_acts = over_x(partial_acts)
    rot_grads = lax.all_gather(grads, "y", axis=0, tiled=True)
    ids = lax.dynamic_index_in_dim(doc_ids.reshape(32, 2, 16), c, 1, keepdims=False)
    docs = score(rot_grads, precond, swap(precond), rot_acts, ids)
    total = jnp.sum(spread(docs[:, 0, :DOCS].reshape(1, 2 * DOCS), ALL, 256), axis=0)
    return total.reshape(2, DOCS).T


def solution(mesh):
    finer = Mesh(mesh.devices.reshape(4, 8, 4, 2), ALL)
    in_specs = (
        P(WIDE, NARROW),
        P(WIDE, None),
        P(NARROW, WIDE),
        P(WIDE, NARROW),
        P(NARROW, WIDE),
        P(None, NARROW, WIDE),
        P(),
    )
    return jax.shard_map(
        shards, mesh=finer, in_specs=in_specs, out_specs=P(), check_vma=False
    )
```

```python
import functools

import jax
import jax.numpy as jnp
from jax import lax
from jax.experimental import pallas as pl
from jax.experimental.pallas import tpu as pltpu
from jax.sharding import Mesh
from jax.sharding import PartitionSpec as P

WIDE = ("y", "z")
NARROW = ("x", "c")
ALL = ("y", "z", "x", "c")
SIZE = {"y": 4, "z": 8, "x": 4, "c": 2}
DOCS = 64
DAMPING = 0.1
F32 = jnp.float32
BF16 = jnp.bfloat16
STEP = 512
SPLIT = 3584


def shift(value, axis, hops):
    size = SIZE[axis]
    return lax.ppermute(value, axis, [(i, (i + hops) % size) for i in range(size)])


def ring(chunk, axis):
    size = SIZE[axis]
    half = size // 2
    got = [(0, 0, chunk)]
    ahead = back = chunk
    for step in range(1, half):
        ahead, back = shift(ahead, axis, 1), shift(back, axis, -1)
        got += [(step, 0, ahead), (size - step, 0, back)]
    cut = chunk.shape[1] // 2
    got += [(half, 0, shift(ahead[:, :cut], axis, 1)), (half, cut, shift(back[:, cut:], axis, -1))]
    return got


def spread(value, axes, size):
    return lax.all_to_all(jnp.broadcast_to(value[None], (size,) + value.shape), axes, 0, 0)


def join_kernel(places, rows, here, *refs):
    chunks, (basis, out, same) = refs[: len(places)], refs[len(places) :]
    same[...] = basis[...]
    for back, chunk in zip(places, chunks):
        row = pl.multiple_of(lax.rem(here[0] + len(places) - back, len(places)) * rows, rows)
        out[pl.ds(row, rows), :] = chunk[...]


PLACES = (0, 1, 3, 2)


def direct(value):
    return [value] + [shift(value, "y", back) for back in PLACES[1:]]


def join(value, basis, here):
    rows, cols = value.shape
    return pl.pallas_call(
        functools.partial(join_kernel, PLACES, rows),
        out_shape=(jax.ShapeDtypeStruct((4 * rows, cols), BF16), jax.ShapeDtypeStruct(basis.shape, BF16)),
        in_specs=[pl.BlockSpec(memory_space=pltpu.SMEM)] + [pl.BlockSpec(memory_space=pltpu.VMEM)] * 5,
        out_specs=(pl.BlockSpec(memory_space=pltpu.VMEM), pl.BlockSpec(memory_space=pltpu.VMEM)),
        cost_estimate=pl.CostEstimate(flops=0, bytes_accessed=16 * rows * cols, transcendentals=0),
        name="join",
    )(here, *direct(value), basis)


def project_kernel(here, own, other, first, second, third, left, right, out):
    for half, rows in enumerate((own, other)):
        total = 0.0
        for back, parts in ((0, (first,)), (1, (second,)), (3, (third,)), (2, (left, right))):
            slot = pl.multiple_of(lax.rem(here[0] + 4 - back, 4) * 256, 256)
            part = rows[:, pl.ds(slot, 256)]
            sums = [jnp.dot(part, basis[...], preferred_element_type=F32) for basis in parts]
            total += sums[0] if len(sums) == 1 else jnp.concatenate(sums, axis=1)
        out[:, half] = total.astype(BF16).reshape(8, 16, 1024)


def project(own, other, bases, here):
    vmem = pl.BlockSpec(memory_space=pltpu.VMEM)
    return pl.pallas_call(
        project_kernel,
        out_shape=jax.ShapeDtypeStruct((8, 2, 16, 1024), BF16),
        in_specs=[pl.BlockSpec(memory_space=pltpu.SMEM)] + [vmem] * 7,
        out_specs=vmem,
        cost_estimate=pl.CostEstimate(flops=75 * 2**29, bytes_accessed=2**22, transcendentals=0),
        compiler_params=pltpu.CompilerParams(vmem_limit_bytes=16 << 20),
        name="project",
    )(here, own, other, *bases)


def damp_kernel(queries, eigenvalues, _, out):
    damped = eigenvalues[...].astype(F32) + DAMPING
    for q in range(2):
        out[q] = (queries[q].astype(F32) / damped).astype(BF16)


def damp(queries, eigenvalues, ready):
    count, rows, cols = queries.shape
    return pl.pallas_call(
        damp_kernel,
        grid=(rows // 128,),
        out_shape=jax.ShapeDtypeStruct((count, rows, cols), BF16),
        in_specs=[
            pl.BlockSpec((count, 128, cols), lambda i: (0, i, 0)),
            pl.BlockSpec((128, cols), lambda i: (i, 0)),
            pl.BlockSpec(memory_space=pl.ANY),
        ],
        out_specs=pl.BlockSpec((count, 128, cols), lambda i: (0, i, 0)),
        cost_estimate=pl.CostEstimate(
            flops=2 * count * rows * cols, bytes_accessed=10 * rows * cols, transcendentals=0
        ),
        compiler_params=pltpu.CompilerParams(vmem_limit_bytes=56 << 20),
        name="damp",
    )(queries, eigenvalues, ready)


def rotate_kernel(places, axis, spans, summed, here, *refs):
    count = len(places)
    chunks, bases, refs = refs[:count], refs[count : count + len(spans)], refs[count + len(spans) :]
    before, (out, lhs, rhs, total, chunk_sems, basis_sems) = refs[:summed], refs[-6:]
    steps = rhs.shape[0]
    loads = []

    for n, ((back, first, width), chunk) in enumerate(zip(places, chunks)):
        if axis == "y":
            into = lhs.at[lax.rem(here[0] + 4 - back, 4), :, :, pl.ds(first, width)]
            loads.append(pltpu.make_async_copy(chunk, into, chunk_sems.at[n]))
        else:
            loads.append(pltpu.make_async_copy(chunk.at[:, back], lhs.at[back], chunk_sems.at[n]))

    def basis_load(basis, row, k):
        return pltpu.make_async_copy(basis.at[pl.ds(row, STEP)], rhs.at[k], basis_sems.at[k])

    for n in loads:
        n.start()
    k = 0
    for basis, (first, last) in zip(bases, spans):
        for row in range(first, last, STEP):
            basis_load(basis, row, k).start()
            k += 1
    total[...] = before[0][...] if summed else jnp.zeros_like(total)
    for n in loads:
        n.wait()

    @pl.loop(0, steps)
    def _(k):
        basis_load(bases[0], 0, k).wait()
        part = lhs[:, :, :, pl.ds(pl.multiple_of(k * STEP, STEP), STEP)].reshape(512, STEP)
        total[...] += jnp.dot(part, rhs[k], preferred_element_type=F32)

    out[...] = total[...].astype(out.dtype)


def rotate(chunks, axis, bases, here, dtype, ready, before=()):
    spans = [span for _, span in bases]
    depth, cols = sum(last - first for first, last in spans), bases[0][0].shape[1]
    places = [(back, first, chunk.shape[-1]) for back, first, chunk in chunks]
    count = 512
    steps = depth // STEP
    copies = len(places)
    return pl.pallas_call(
        functools.partial(rotate_kernel, places, axis, spans, len(before)),
        out_shape=jax.ShapeDtypeStruct((count, cols), dtype),
        in_specs=[pl.BlockSpec(memory_space=pltpu.SMEM)]
        + [pl.BlockSpec(memory_space=pl.ANY)] * len(places)
        + [pl.BlockSpec(memory_space=pltpu.HBM)] * len(bases)
        + [pl.BlockSpec(memory_space=pltpu.VMEM)] * len(before)
        + [pl.BlockSpec(memory_space=pl.ANY)] * len(ready),
        out_specs=pl.BlockSpec(memory_space=pltpu.VMEM),
        scratch_shapes=[
            pltpu.VMEM((4, 8, 16, depth), BF16),
            pltpu.VMEM((steps, STEP, cols), BF16),
            pltpu.VMEM((count, cols), F32),
            pltpu.SemaphoreType.DMA((copies,)),
            pltpu.SemaphoreType.DMA((steps,)),
        ],
        cost_estimate=pl.CostEstimate(
            flops=(4 if axis == "y" else 4) * 2 * count * depth * cols,
            bytes_accessed=2 * (count * depth + depth * cols + count * cols),
            transcendentals=0,
        ),
        compiler_params=pltpu.CompilerParams(vmem_limit_bytes=48 << 20),
        name="rotate_" + axis,
    )(here, *[chunk for _, _, chunk in chunks], *[basis for basis, _ in bases], *before, *ready)


def score_kernel(grads, own, other, acts, ids, out):
    half = own.shape[1]
    mixed = jnp.dot(grads[:, :half], own[0], preferred_element_type=F32)
    mixed += jnp.dot(grads[:, half:], other[0], preferred_element_type=F32)
    token = jnp.sum(mixed * acts[...].astype(F32), axis=1, keepdims=True)
    docs = lax.broadcasted_iota(jnp.int32, (token.shape[0], 128), 1)
    out[0] = jnp.sum(jnp.where(ids[...] == docs, token, 0.0), axis=0, keepdims=True)


def score(grads, own, other, acts, ids):
    tokens, cols = acts.shape
    count, half, _ = own.shape
    return pl.pallas_call(
        score_kernel,
        grid=(count,),
        out_shape=jax.ShapeDtypeStruct((count, 1, 128), F32),
        in_specs=[
            pl.BlockSpec((tokens, 2 * half), lambda q: (0, 0)),
            pl.BlockSpec((1, half, cols), lambda q: (q, 0, 0)),
            pl.BlockSpec((1, half, cols), lambda q: (q, 0, 0)),
            pl.BlockSpec((tokens, cols), lambda q: (0, 0)),
            pl.BlockSpec((tokens, 1), lambda q: (0, 0)),
        ],
        out_specs=pl.BlockSpec((1, 1, 128), lambda q: (q, 0, 0)),
        cost_estimate=pl.CostEstimate(
            flops=4 * count * tokens * half * cols,
            bytes_accessed=2 * (2 * tokens * half + 2 * count * half * cols + tokens * cols),
            transcendentals=0,
        ),
        compiler_params=pltpu.CompilerParams(vmem_limit_bytes=56 << 20),
        name="score",
    )(grads, own, other, acts, ids.reshape(tokens, 1))


def after_kernel(value, ready, out):
    pass


def after(value, ready):
    anywhere = pl.BlockSpec(memory_space=pl.ANY)
    return pl.pallas_call(
        after_kernel,
        out_shape=jax.ShapeDtypeStruct(value.shape, value.dtype),
        in_specs=[anywhere, anywhere],
        out_specs=anywhere,
        input_output_aliases={0: 0},
        name="after",
    )(value, ready)


def over_x(partial):
    rows, cols = partial.shape
    parts = lax.all_to_all(partial.reshape(4, rows // 4, cols), "x", 0, 0)
    share = jnp.sum(parts.astype(F32), axis=0).astype(BF16)
    return spread(share, "x", 4).reshape(rows, cols)


def swap(value):
    return shift(value, "c", 1)


def shards(activations, out_grads, basis_in, basis_out, eigenvalues, queries, doc_ids):
    y, z, c = (lax.axis_index(axis) for axis in "yzc")
    here = jnp.stack([y, z])
    other_in = swap(basis_in)
    mine = lax.dynamic_slice_in_dim(activations, c * 16, 16)
    theirs = swap(lax.dynamic_slice_in_dim(activations, (1 - c) * 16, 16))
    extra = SPLIT - mine.shape[1]
    first_low, basis_out = join(theirs[:, extra:], basis_out, here)
    low = first_low
    low = lax.all_gather(low, "z", axis=0, tiled=True).reshape(8, 4, 16, -1)
    cut = basis_out.shape[1] // 2
    bases = [basis_out, shift(basis_out, "y", 1), shift(basis_out, "y", -1)]
    precond = damp(queries, eigenvalues, first_low)
    bases += [shift(after(basis_out[:, :cut], precond), "y", 2), shift(basis_out[:, cut:], "y", -2)]
    rows = lax.dynamic_slice_in_dim(out_grads, c * 16, 16).reshape(16, 4, 8, 256)
    rows = rows.transpose(2, 0, 1, 3).reshape(8, 16, 1024)
    mine = jnp.concatenate([mine, theirs[:, :extra]], axis=1)
    copies = jnp.broadcast_to(mine[None], (8,) + mine.shape)
    sent = lax.all_to_all(jnp.concatenate([copies, rows], axis=2), "z", 0, 0)
    high = sent[:, :, :SPLIT].reshape(128, -1)
    rows = sent[:, :, SPLIT:].reshape(128, -1)
    half = basis_in.shape[0]
    high_bases = ((basis_in, (0, half)), (other_in, (0, extra)))[: 1 + (extra > 0)]
    parts = lax.all_to_all(project(rows, swap(rows), bases, here), "z", 0, 0)
    partial_acts = rotate([(back, first, chunk.reshape(8, 16, -1)) for back, first, chunk in ring(high, "y")], "y", high_bases, here, F32, (parts, low))
    grads = jnp.sum(parts.astype(F32), axis=0).astype(BF16)
    grads = jnp.concatenate([grads[0], swap(grads[1])], axis=1)
    copies = jnp.broadcast_to(grads[None], (8,) + grads.shape)
    grads = lax.all_to_all(copies, "z", 0, 0).reshape(128, 2048)
    low_bases = ((other_in, (extra, half)),)
    partial_acts = rotate([(y, 0, low) for y in range(4)], "z", low_bases, here, BF16, (copies,), (partial_acts,))
    grads = after(grads, partial_acts)
    rot_acts = over_x(partial_acts)
    rot_grads = lax.all_gather(grads, "y", axis=0, tiled=True)
    ids = lax.dynamic_index_in_dim(doc_ids.reshape(32, 2, 16), c, 1, keepdims=False)
    docs = score(rot_grads, precond, swap(precond), rot_acts, ids)
    total = jnp.sum(spread(docs[:, 0, :DOCS].reshape(1, 2 * DOCS), ALL, 256), axis=0)
    return total.reshape(2, DOCS).T


def solution(mesh):
    finer = Mesh(mesh.devices.reshape(4, 8, 4, 2), ALL)
    in_specs = (
        P(WIDE, NARROW),
        P(WIDE, None),
        P(NARROW, WIDE),
        P(WIDE, NARROW),
        P(NARROW, WIDE),
        P(None, NARROW, WIDE),
        P(),
    )
    return jax.shard_map(
        shards, mesh=finer, in_specs=in_specs, out_specs=P(), check_vma=False
    )
```

```python
import functools

import jax
import jax.numpy as jnp
from jax import lax
from jax.experimental import pallas as pl
from jax.experimental.pallas import tpu as pltpu
from jax.sharding import Mesh
from jax.sharding import PartitionSpec as P

WIDE = ("y", "z")
NARROW = ("x", "c")
ALL = ("y", "z", "x", "c")
SIZE = {"y": 4, "z": 8, "x": 4, "c": 2}
DOCS = 64
DAMPING = 0.1
F32 = jnp.float32
BF16 = jnp.bfloat16
STEP = 896
SPLIT = 3584


def shift(value, axis, hops):
    size = SIZE[axis]
    return lax.ppermute(value, axis, [(i, (i + hops) % size) for i in range(size)])


def ring(chunk, axis):
    size = SIZE[axis]
    half = size // 2
    got = [(0, 0, chunk)]
    ahead = back = chunk
    for step in range(1, half):
        ahead, back = shift(ahead, axis, 1), shift(back, axis, -1)
        got += [(step, 0, ahead), (size - step, 0, back)]
    cut = chunk.shape[1] // 2
    got += [(half, 0, shift(ahead[:, :cut], axis, 1)), (half, cut, shift(back[:, cut:], axis, -1))]
    return got


def spread(value, axes, size):
    return lax.all_to_all(jnp.broadcast_to(value[None], (size,) + value.shape), axes, 0, 0)


def join_kernel(places, rows, here, *refs):
    chunks, (basis, out, same) = refs[: len(places)], refs[len(places) :]
    same[...] = basis[...]
    for back, chunk in zip(places, chunks):
        row = pl.multiple_of(lax.rem(here[0] + len(places) - back, len(places)) * rows, rows)
        out[pl.ds(row, rows), :] = chunk[...]


PLACES = (0, 1, 3, 2)


def direct(value):
    return [value] + [shift(value, "y", back) for back in PLACES[1:]]


def join(value, basis, here):
    rows, cols = value.shape
    return pl.pallas_call(
        functools.partial(join_kernel, PLACES, rows),
        out_shape=(jax.ShapeDtypeStruct((4 * rows, cols), BF16), jax.ShapeDtypeStruct(basis.shape, BF16)),
        in_specs=[pl.BlockSpec(memory_space=pltpu.SMEM)] + [pl.BlockSpec(memory_space=pltpu.VMEM)] * 5,
        out_specs=(pl.BlockSpec(memory_space=pltpu.VMEM), pl.BlockSpec(memory_space=pltpu.VMEM)),
        cost_estimate=pl.CostEstimate(flops=0, bytes_accessed=16 * rows * cols, transcendentals=0),
        name="join",
    )(here, *direct(value), basis)


def project_kernel(here, own, other, first, second, third, left, right, out):
    for half, rows in enumerate((own, other)):
        total = 0.0
        for back, parts in ((0, (first,)), (1, (second,)), (3, (third,)), (2, (left, right))):
            slot = pl.multiple_of(lax.rem(here[0] + 4 - back, 4) * 256, 256)
            part = rows[:, pl.ds(slot, 256)]
            sums = [jnp.dot(part, basis[...], preferred_element_type=F32) for basis in parts]
            total += sums[0] if len(sums) == 1 else jnp.concatenate(sums, axis=1)
        out[:, half] = total.astype(BF16).reshape(8, 16, 1024)


def project(own, other, bases, here):
    vmem = pl.BlockSpec(memory_space=pltpu.VMEM)
    return pl.pallas_call(
        project_kernel,
        out_shape=jax.ShapeDtypeStruct((8, 2, 16, 1024), BF16),
        in_specs=[pl.BlockSpec(memory_space=pltpu.SMEM)] + [vmem] * 7,
        out_specs=vmem,
        cost_estimate=pl.CostEstimate(flops=75 * 2**29, bytes_accessed=2**22, transcendentals=0),
        compiler_params=pltpu.CompilerParams(vmem_limit_bytes=16 << 20),
        name="project",
    )(here, own, other, *bases)


def damp_kernel(queries, eigenvalues, _, out):
    damped = eigenvalues[...].astype(F32) + DAMPING
    for q in range(2):
        out[q] = (queries[q].astype(F32) / damped).astype(BF16)


def damp(queries, eigenvalues, ready):
    count, rows, cols = queries.shape
    return pl.pallas_call(
        damp_kernel,
        grid=(rows // 128,),
        out_shape=jax.ShapeDtypeStruct((count, rows, cols), BF16),
        in_specs=[
            pl.BlockSpec((count, 128, cols), lambda i: (0, i, 0)),
            pl.BlockSpec((128, cols), lambda i: (i, 0)),
            pl.BlockSpec(memory_space=pl.ANY),
        ],
        out_specs=pl.BlockSpec((count, 128, cols), lambda i: (0, i, 0)),
        cost_estimate=pl.CostEstimate(
            flops=2 * count * rows * cols, bytes_accessed=10 * rows * cols, transcendentals=0
        ),
        compiler_params=pltpu.CompilerParams(vmem_limit_bytes=56 << 20),
        name="damp",
    )(queries, eigenvalues, ready)


def rotate_kernel(places, axis, spans, summed, here, *refs):
    count = len(places)
    chunks, bases, refs = refs[:count], refs[count : count + len(spans)], refs[count + len(spans) :]
    before, (out, lhs, rhs, total, chunk_sems, basis_sems) = refs[:summed], refs[-6:]
    steps = rhs.shape[0]
    loads = []

    for n, ((back, first, width), chunk) in enumerate(zip(places, chunks)):
        if axis == "y":
            into = lhs.at[lax.rem(here[0] + 4 - back, 4), :, :, pl.ds(first, width)]
            loads.append(pltpu.make_async_copy(chunk, into, chunk_sems.at[n]))
        else:
            loads.append(pltpu.make_async_copy(chunk.at[:, back], lhs.at[back], chunk_sems.at[n]))

    def basis_load(basis, row, k):
        return pltpu.make_async_copy(basis.at[pl.ds(row, STEP)], rhs.at[k], basis_sems.at[k])

    for n in loads:
        n.start()
    k = 0
    for basis, (first, last) in zip(bases, spans):
        for row in range(first, last, STEP):
            basis_load(basis, row, k).start()
            k += 1
    total[...] = before[0][...] if summed else jnp.zeros_like(total)
    for n in loads:
        n.wait()

    @pl.loop(0, steps)
    def _(k):
        basis_load(bases[0], 0, k).wait()
        part = lhs[:, :, :, pl.ds(pl.multiple_of(k * STEP, STEP), STEP)].reshape(512, STEP)
        total[...] += jnp.dot(part, rhs[k], preferred_element_type=F32)

    out[...] = total[...].astype(out.dtype)


def rotate(chunks, axis, bases, here, dtype, ready, before=()):
    spans = [span for _, span in bases]
    depth, cols = sum(last - first for first, last in spans), bases[0][0].shape[1]
    places = [(back, first, chunk.shape[-1]) for back, first, chunk in chunks]
    count = 512
    steps = depth // STEP
    copies = len(places)
    return pl.pallas_call(
        functools.partial(rotate_kernel, places, axis, spans, len(before)),
        out_shape=jax.ShapeDtypeStruct((count, cols), dtype),
        in_specs=[pl.BlockSpec(memory_space=pltpu.SMEM)]
        + [pl.BlockSpec(memory_space=pl.ANY)] * len(places)
        + [pl.BlockSpec(memory_space=pltpu.HBM)] * len(bases)
        + [pl.BlockSpec(memory_space=pltpu.VMEM)] * len(before)
        + [pl.BlockSpec(memory_space=pl.ANY)] * len(ready),
        out_specs=pl.BlockSpec(memory_space=pltpu.VMEM),
        scratch_shapes=[
            pltpu.VMEM((4, 8, 16, depth), BF16),
            pltpu.VMEM((steps, STEP, cols), BF16),
            pltpu.VMEM((count, cols), F32),
            pltpu.SemaphoreType.DMA((copies,)),
            pltpu.SemaphoreType.DMA((steps,)),
        ],
        cost_estimate=pl.CostEstimate(
            flops=(4 if axis == "y" else 4) * 2 * count * depth * cols,
            bytes_accessed=2 * (count * depth + depth * cols + count * cols),
            transcendentals=0,
        ),
        compiler_params=pltpu.CompilerParams(vmem_limit_bytes=48 << 20),
        name="rotate_" + axis,
    )(here, *[chunk for _, _, chunk in chunks], *[basis for basis, _ in bases], *before, *ready)


def score_kernel(grads, own, other, acts, ids, out):
    half = own.shape[1]
    mixed = jnp.dot(grads[:, :half], own[0], preferred_element_type=F32)
    mixed += jnp.dot(grads[:, half:], other[0], preferred_element_type=F32)
    token = jnp.sum(mixed * acts[...].astype(F32), axis=1, keepdims=True)
    docs = lax.broadcasted_iota(jnp.int32, (token.shape[0], 128), 1)
    out[0] = jnp.sum(jnp.where(ids[...] == docs, token, 0.0), axis=0, keepdims=True)


def score(grads, own, other, acts, ids):
    tokens, cols = acts.shape
    count, half, _ = own.shape
    return pl.pallas_call(
        score_kernel,
        grid=(count,),
        out_shape=jax.ShapeDtypeStruct((count, 1, 128), F32),
        in_specs=[
            pl.BlockSpec((tokens, 2 * half), lambda q: (0, 0)),
            pl.BlockSpec((1, half, cols), lambda q: (q, 0, 0)),
            pl.BlockSpec((1, half, cols), lambda q: (q, 0, 0)),
            pl.BlockSpec((tokens, cols), lambda q: (0, 0)),
            pl.BlockSpec((tokens, 1), lambda q: (0, 0)),
        ],
        out_specs=pl.BlockSpec((1, 1, 128), lambda q: (q, 0, 0)),
        cost_estimate=pl.CostEstimate(
            flops=4 * count * tokens * half * cols,
            bytes_accessed=2 * (2 * tokens * half + 2 * count * half * cols + tokens * cols),
            transcendentals=0,
        ),
        compiler_params=pltpu.CompilerParams(vmem_limit_bytes=56 << 20),
        name="score",
    )(grads, own, other, acts, ids.reshape(tokens, 1))


def after_kernel(value, ready, out):
    pass


def after(value, ready):
    anywhere = pl.BlockSpec(memory_space=pl.ANY)
    return pl.pallas_call(
        after_kernel,
        out_shape=jax.ShapeDtypeStruct(value.shape, value.dtype),
        in_specs=[anywhere, anywhere],
        out_specs=anywhere,
        input_output_aliases={0: 0},
        name="after",
    )(value, ready)


def over_x(partial):
    rows, cols = partial.shape
    parts = lax.all_to_all(partial.reshape(4, rows // 4, cols), "x", 0, 0)
    share = jnp.sum(parts.astype(F32), axis=0).astype(BF16)
    return spread(share, "x", 4).reshape(rows, cols)


def swap(value):
    return shift(value, "c", 1)


def shards(activations, out_grads, basis_in, basis_out, eigenvalues, queries, doc_ids):
    y, z, c = (lax.axis_index(axis) for axis in "yzc")
    here = jnp.stack([y, z])
    other_in = swap(basis_in)
    mine = lax.dynamic_slice_in_dim(activations, c * 16, 16)
    theirs = swap(lax.dynamic_slice_in_dim(activations, (1 - c) * 16, 16))
    extra = SPLIT - mine.shape[1]
    first_low, basis_out = join(theirs[:, extra:], basis_out, here)
    low = first_low
    low = lax.all_gather(low, "z", axis=0, tiled=True).reshape(8, 4, 16, -1)
    cut = basis_out.shape[1] // 2
    bases = [basis_out, shift(basis_out, "y", 1), shift(basis_out, "y", -1)]
    precond = damp(queries, eigenvalues, first_low)
    bases += [shift(after(basis_out[:, :cut], precond), "y", 2), shift(basis_out[:, cut:], "y", -2)]
    rows = lax.dynamic_slice_in_dim(out_grads, c * 16, 16).reshape(16, 4, 8, 256)
    rows = rows.transpose(2, 0, 1, 3).reshape(8, 16, 1024)
    mine = jnp.concatenate([mine, theirs[:, :extra]], axis=1)
    copies = jnp.broadcast_to(mine[None], (8,) + mine.shape)
    sent = lax.all_to_all(jnp.concatenate([copies, rows], axis=2), "z", 0, 0)
    high = sent[:, :, :SPLIT].reshape(128, -1)
    rows = sent[:, :, SPLIT:].reshape(128, -1)
    half = basis_in.shape[0]
    high_bases = ((basis_in, (0, half)), (other_in, (0, extra)))[: 1 + (extra > 0)]
    parts = lax.all_to_all(project(rows, swap(rows), bases, here), "z", 0, 0)
    partial_acts = rotate([(back, first, chunk.reshape(8, 16, -1)) for back, first, chunk in ring(high, "y")], "y", high_bases, here, F32, (parts, low))
    grads = jnp.sum(parts.astype(F32), axis=0).astype(BF16)
    grads = jnp.concatenate([grads[0], swap(grads[1])], axis=1)
    copies = jnp.broadcast_to(grads[None], (8,) + grads.shape)
    grads = lax.all_to_all(copies, "z", 0, 0).reshape(128, 2048)
    low_bases = ((other_in, (extra, half)),)
    partial_acts = rotate([(y, 0, low) for y in range(4)], "z", low_bases, here, BF16, (copies,), (partial_acts,))
    grads = after(grads, partial_acts)
    rot_acts = over_x(partial_acts)
    rot_grads = lax.all_gather(grads, "y", axis=0, tiled=True)
    ids = lax.dynamic_index_in_dim(doc_ids.reshape(32, 2, 16), c, 1, keepdims=False)
    docs = score(rot_grads, precond, swap(precond), rot_acts, ids)
    total = jnp.sum(spread(docs[:, 0, :DOCS].reshape(1, 2 * DOCS), ALL, 256), axis=0)
    return total.reshape(2, DOCS).T


def solution(mesh):
    finer = Mesh(mesh.devices.reshape(4, 8, 4, 2), ALL)
    in_specs = (
        P(WIDE, NARROW),
        P(WIDE, None),
        P(NARROW, WIDE),
        P(WIDE, NARROW),
        P(NARROW, WIDE),
        P(None, NARROW, WIDE),
        P(),
    )
    return jax.shard_map(
        shards, mesh=finer, in_specs=in_specs, out_specs=P(), check_vma=False
    )
```
